1024 devices in a mesh: depth: 128 (over z_hi, y, x), outer: 8 (over z_lo, core).
Axes of the slice: x: 8, y: 8, z: 8 (z_hi: 2, z_lo: 4; z = z_hi * 4 + z_lo), core: 2. Of those that a mesh axis runs over, the one named last changes fastest.
Arguments:
- density: float32 [8192, 16, 1024], P(('depth', 'outer')), may hold values from -16 to 16
- materials: int32 [8192, 4, 256], P(('depth', 'outer')), may hold values from 0 to 15
- colors: float32 [3, 16], replicated, may hold values from 0.1 to 1
- opacity: float32 [16], replicated, may hold values from 2e-05 to 0.003
Outputs:
- picture: float32 [3, 16384], P(None, ('depth', 'outer'))
The draws below stay inside these ranges and needn't reach their ends.
All inputs are finite; a program needn't handle non-finite values.
Results may differ from the reference program's by a relative error of at most 0.0003.
Values sent between devices are 32-bit elements; how exact they have to be, the bound alone decides.
No kernel may reach another device: no remote copies, remote signals or barrier semaphores. Data moves between devices by JAX's collectives and lax.ppermute only.
A program may use at most 64 MiB of HBM per device.

```python
import math
import jax
import jax.numpy as jnp
import numpy as np
from jax import lax

NX = 1024
NY = 16
PZ = 8
MATS = 16
NZ = 8192


def set_ends(values, own_key, smallest, largest):
    longest = values.shape.index(max(values.shape))
    spots = []
    for shift in (0, 1):
        where = [jax.random.randint(jax.random.fold_in(own_key, axis), (), 0, length) for axis, length in enumerate(values.shape)]
        where[longest] = (where[longest] + shift) % values.shape[longest]
        spots.append(tuple(where))
    return values.at[spots[0]].set(smallest).at[spots[1]].set(largest)


def block_levels(own_key, shape, pieces, least, high):
    level, own = 1.0, jax.random.fold_in(own_key, 6)
    for axis_at, blocks in pieces:
        steps = jnp.exp(jax.random.uniform(jax.random.fold_in(own, axis_at), (blocks,), jnp.float32, least / len(pieces), high / len(pieces)))
        level = level * jnp.repeat(steps, shape[axis_at] // blocks).reshape([-1 if axis == axis_at else 1 for axis in range(len(shape))])
    return level


def cumulative_ranks(amount, slope):
    weights = [(1 << 20) // math.isqrt(standing ** slope) + 1 for standing in range(1, amount + 1)]
    scale = 1 + sum(weights) // (1 << 30)
    return np.cumsum(np.array([max(1, weight // scale) for weight in weights]))


def skewed_ids(stream_key, shape, amount, lean):
    listing = cumulative_ranks(amount, lean)
    pick = jax.random.randint(jax.random.fold_in(stream_key, 1), shape, 0, int(listing[amount - 1]))
    rank = jnp.searchsorted(jnp.asarray(listing, jnp.int32), pick, side="right")
    return jax.random.permutation(jax.random.fold_in(stream_key, 2), amount)[rank].astype(jnp.int32)


def centred(stream_key, shape, width, limit, pieces=(), kind=jnp.bfloat16):
    array = width * jax.random.normal(stream_key, shape, jnp.float32)
    if pieces:
        array = array * block_levels(stream_key, shape, pieces, -0.22, 0.18)
    return jnp.clip(array, -limit, limit).astype(kind)


def setup_inputs(seed: int = 0) -> dict:
    streams_of = jax.random.split(jax.random.key(seed), 5)
    return {
        "density": centred(streams_of[0], (NZ, NY, NX), 4.0, 16.0, ((0, 1024),), jnp.float32),
        "materials": set_ends(skewed_ids(streams_of[1], (NZ, NY // 4, NX // 4), MATS, 2), jax.random.fold_in(streams_of[1], 3), 0, MATS - 1).astype(jnp.int32),
        "colors": jnp.clip(jax.random.uniform(streams_of[2], (3, MATS), jnp.float32, 0.1, 1.0), 0.1, 1.0),
        "opacity": jnp.clip(jnp.exp(jax.random.uniform(streams_of[3], (MATS,), jnp.float32, math.log(1.9999999494757503e-05), math.log(0.003))), 1.9999999494757503e-05, 0.003),
    }


LIGHT_DIR = (0.64, 0.48, 0.6)

def smooth_pass(volume, inside):
    padded = jnp.pad(volume, 1)
    beside = padded[2:, 1:-1, 1:-1] + padded[:-2, 1:-1, 1:-1]
    beside = beside + padded[1:-1, 2:, 1:-1] + padded[1:-1, :-2, 1:-1]
    beside = beside + padded[1:-1, 1:-1, 2:] + padded[1:-1, 1:-1, :-2]
    return jnp.where(inside, 0.25 * volume + 0.125 * beside, 0.0)

def derive(volume, axis):
    length = volume.shape[axis]
    widths = [(0, 0), (0, 0), (0, 0)]
    widths[axis] = (2, 2)
    padded = jnp.pad(volume, widths)

    def part(offset):
        return lax.slice_in_dim(padded, offset, offset + length, 1, axis)
    return (part(3) - part(1) + 2.0 * (part(4) - part(0))) / 10.0

def render_slab(extended, labels, first_plane, total_planes, colors, opacity):
    planes = extended.shape[0]
    depth_own = planes - 8
    global_plane = first_plane - 4 + jnp.arange(planes, dtype=jnp.int32)
    inside = ((global_plane >= 0) & (global_plane < total_planes))[:, None, None]
    volume = jnp.where(inside, extended.astype(jnp.float32), 0.0)
    volume = smooth_pass(volume, inside)
    volume = smooth_pass(volume, inside)
    smoothed = volume[2:depth_own + 6]
    grad_depth = (smoothed[3:depth_own + 3] - smoothed[1:depth_own + 1] + 2.0 * (smoothed[4:depth_own + 4] - smoothed[0:depth_own])) / 10.0
    center = smoothed[2:depth_own + 2]
    grad_rows = derive(center, 1)
    grad_cols = derive(center, 2)
    facing = LIGHT_DIR[0] * grad_depth + LIGHT_DIR[1] * grad_rows + LIGHT_DIR[2] * grad_cols
    length_sq = grad_depth * grad_depth + grad_rows * grad_rows + grad_cols * grad_cols + 1.0
    shading = 0.1 + 0.9 * jnp.abs(facing) / jnp.sqrt(length_sq)
    fine_labels = jnp.repeat(jnp.repeat(labels, 4, axis=1), 4, axis=2)
    alphas = jnp.zeros(center.shape, jnp.float32)
    tinted = jnp.zeros((3,) + center.shape, jnp.float32)
    for label_id in range(colors.shape[1]):
        chosen = fine_labels == label_id
        alphas = jnp.where(chosen, opacity[label_id], alphas)
        tinted = jnp.where(chosen[None], colors[:, label_id][:, None, None, None], tinted)
    alphas = alphas * jax.nn.sigmoid(2.0 * center)
    emitted = tinted * (alphas * shading)[None]
    radiance = jnp.zeros((3,) + center.shape[1:], jnp.float32)
    transmit = jnp.ones(center.shape[1:], jnp.float32)
    for plane_at in range(depth_own):
        radiance = radiance + transmit * emitted[:, plane_at]
        transmit = transmit * (1.0 - alphas[plane_at])
    return (radiance, transmit)

def reference(density, materials, colors, opacity):
    padded = jnp.pad(density, ((4, 4), (0, 0), (0, 0)))
    blocks = NZ // PZ

    def advance(carry, block_at):
        radiance, transmit = carry
        start = (block_at * PZ).astype(jnp.int32)
        extended = lax.dynamic_slice_in_dim(padded, start, PZ + 8, 0)
        labels = lax.dynamic_slice_in_dim(materials, start, PZ, 0)
        slab_light, slab_pass = render_slab(extended, labels, start, NZ, colors, opacity)
        return ((radiance + transmit * slab_light, transmit * slab_pass), None)
    init = (jnp.zeros((3, NY, NX), jnp.float32), jnp.ones((NY, NX), jnp.float32))
    (radiance, transmit), unused = lax.scan(advance, init, jnp.arange(blocks, dtype=jnp.int32))
    return 1.0 - jnp.exp(-4.0 * radiance.reshape(3, NY * NX))
```

```python
import jax
import jax.numpy as jnp
from jax import lax
from jax.experimental import pallas as pl
from jax.experimental.pallas import tpu as pltpu
from jax.sharding import Mesh, PartitionSpec as P

LIGHT_DIR = (0.64, 0.48, 0.6)
AXES = ("zh", "y", "x", "zl", "c")
LANES, SUBS = 128, 8
TILES = 8
PITCH = 24
ROWS = PITCH * TILES + SUBS
WIDE = PITCH * (TILES + 2) + SUBS
TILE = (SUBS, LANES)


def iota(axis):
    return lax.broadcasted_iota(jnp.int32, TILE, axis)


def shift_columns(tiles, at, by):
    lane = iota(1)
    if by < 0:
        beside = tiles[at - 1] if at else jnp.zeros(TILE, jnp.float32)
        mixed = jnp.where(lane >= LANES + by, beside, tiles[at])
    else:
        beside = tiles[at + 1] if at + 1 < len(tiles) else jnp.zeros(TILE, jnp.float32)
        mixed = jnp.where(lane < by, beside, tiles[at])
    return pltpu.roll(mixed, (-by) % LANES, 1)


def smooth_planes(source, target, pad, count, scale_of):
    def body(k, carry):
        scale = scale_of(k)
        near, far = 0.25 * scale, 0.125 * scale
        for half in range(2):
            offs = [SUBS + PITCH * t + SUBS * half for t in range(TILES)]
            tiles = [source[k + 1, pl.ds(o, SUBS), :] for o in offs]
            for t, o in enumerate(offs):
                beside = shift_columns(tiles, t, -1) + shift_columns(tiles, t, 1)
                beside += source[k + 1, pl.ds(o - 1, SUBS), :] + source[k + 1, pl.ds(o + 1, SUBS), :]
                beside += source[k, pl.ds(o, SUBS), :] + source[k + 2, pl.ds(o, SUBS), :]
                target[k, pl.ds(o + pad, SUBS), :] = near * tiles[t] + far * beside
        return carry

    lax.fori_loop(0, count, body, 0)


def transposed_groups(values):
    group = iota(1) // 16
    values = list(values)
    for bit in (1, 2, 4):
        low = (group & bit) == 0
        for i in range(8):
            if not i & bit:
                a, b = values[i], values[i | bit]
                values[i] = jnp.where(low, a, pltpu.roll(b, 16 * bit, 1))
                values[i | bit] = jnp.where(low, pltpu.roll(a, LANES - 16 * bit, 1), b)
    return values


def take_lanes(values, index):
    return jnp.take_along_axis(values, index, axis=1)


def slab_kernel(colors, opacity, own, low, high, labels, out, raw, once, twice, looked, sems):
    planes = own.shape[0]
    copies = []
    for t in range(TILES):
        cols, rows = pl.ds(LANES * t, LANES), pl.ds(SUBS + PITCH * t, 2 * SUBS)
        for part, (ref, start) in enumerate(((low, 0), (own, 4), (high, 4 + planes))):
            copy = pltpu.make_async_copy(
                ref.at[:, :, cols], raw.at[pl.ds(start, ref.shape[0]), rows, :], sems.at[part, t]
            )
            copy.start()
            copies.append(copy)

    for t in range(TILES + 1):
        gap = pl.ds(PITCH * t, SUBS)
        raw[:, gap, :] = jnp.zeros((raw.shape[0], SUBS, LANES), jnp.float32)
        once[:, gap, :] = jnp.zeros((once.shape[0], SUBS, LANES), jnp.float32)
    for t in range(TILES + 3):
        gap = pl.ds(PITCH * t, SUBS)
        twice[:, gap, :] = jnp.zeros((twice.shape[0], SUBS, LANES), jnp.float32)
    for t in (0, TILES + 1):
        edge = pl.ds(SUBS + PITCH * t, 2 * SUBS)
        twice[:, edge, :] = jnp.zeros((twice.shape[0], 2 * SUBS, LANES), jnp.float32)

    lane, sub = iota(1), iota(0)
    tables = [jnp.zeros(TILE, jnp.float32) for _ in range(4)]
    for m in range(16):
        here = lane == m
        entries = (0.5 * opacity[m], colors[0, m], colors[1, m], colors[2, m])
        tables = [jnp.where(here, e, t) for e, t in zip(entries, tables)]

    def look(p, carry):
        for half in range(2):
            for side in range(2):
                cols = slice(LANES * side, LANES * (side + 1))
                a = jnp.broadcast_to(labels[p, 2 * half : 2 * half + 1, cols], TILE)
                b = jnp.broadcast_to(labels[p, 2 * half + 1 : 2 * half + 2, cols], TILE)
                index = jnp.where(sub < 4, a, b)
                for i, table in enumerate(tables):
                    looked[i, side, 2 * p + half] = take_lanes(table, index)
        return carry

    lax.fori_loop(0, planes, look, 0)

    position = lax.axis_index(AXES[0])
    total = lax.axis_size(AXES[0])
    for name in AXES[1:]:
        position = position * lax.axis_size(name) + lax.axis_index(name)
        total = total * lax.axis_size(name)
    is_first, is_last = position == 0, position == total - 1

    def scale_of(margin):
        def scale(k):
            outside = (is_first & (k < margin)) | (is_last & (k >= margin + planes))
            return jnp.where(outside, 0.0, 1.0)

        return scale

    for copy in copies:
        copy.wait()
    smooth_planes(raw, once, 0, planes + 6, scale_of(3))
    smooth_planes(once, twice, PITCH, planes + 4, scale_of(2))

    def shade(t, carry):
        side = t // 4
        spread = (t % 4) * 32 + lane // 4
        start = pl.multiple_of(PITCH * t, SUBS) + PITCH + SUBS
        layers = [[None] * 4 for _ in range(2)]
        for p in range(planes):
            for half in range(2):
                o = start + SUBS * half

                def at(dz, dy, dt=0):
                    return twice[p + 2 + dz, pl.ds(o + dy + PITCH * dt, SUBS), :]

                center = at(0, 0)
                row = [at(0, 0, -1), center, at(0, 0, 1)]
                depth_g = (at(1, 0) - at(-1, 0)) + 2.0 * (at(2, 0) - at(-2, 0))
                rows_g = (at(0, 1) - at(0, -1)) + 2.0 * (at(0, 2) - at(0, -2))
                cols_g = (shift_columns(row, 1, 1) - shift_columns(row, 1, -1)) + 2.0 * (
                    shift_columns(row, 1, 2) - shift_columns(row, 1, -2)
                )
                facing = (
                    (0.9 * LIGHT_DIR[0]) * depth_g + (0.9 * LIGHT_DIR[1]) * rows_g + (0.9 * LIGHT_DIR[2]) * cols_g
                )
                length = depth_g * depth_g + rows_g * rows_g + cols_g * cols_g + 100.0
                shading = 0.1 + jnp.abs(facing) * lax.rsqrt(length)
                scale, *tint = [take_lanes(looked[i, side, 2 * p + half], spread) for i in range(4)]
                alpha = scale + scale * jnp.tanh(center)
                light = alpha * shading
                if p == 0:
                    layers[half] = [c * light for c in tint] + [1.0 - alpha]
                else:
                    transmit = layers[half][3]
                    light = transmit * light
                    layers[half] = [a + c * light for a, c in zip(layers[half], tint)] + [
                        transmit - transmit * alpha
                    ]
        pieces = []
        for channel in range(4):
            for half in range(2):
                value = layers[half][channel]
                pieces.append(value if channel < 3 else 1.0 - value)
        for g, piece in enumerate(transposed_groups(pieces)):
            out[t, g] = piece
        return carry

    lax.fori_loop(0, TILES, shade, 0)


def over(front, back):
    cover = take_lanes(front, 96 + iota(1) % 32)
    return front + (1.0 - cover) * back


def merge_kernel(parts, out):
    level = [parts[i] for i in range(parts.shape[0])]
    while len(level) > 1:
        level = [over(a, b) for a, b in zip(level[::2], level[1::2])]
    out[0:SUBS, :] = level[0]
    out[SUBS : 2 * SUBS, :] = level[0]


def final_kernel(parts, out):
    lane = lax.broadcasted_iota(jnp.int32, parts.shape, 1)
    value = parts[...]
    step = 1
    while step < parts.shape[0]:
        cover = take_lanes(value, 96 + lane % 32)
        value = value + (1.0 - cover) * pltpu.roll(value, parts.shape[0] - step, 0)
        step *= 2
    value = value[0:SUBS]
    value = jnp.where(lax.axis_index("zh") == 0, value, pltpu.roll(value, LANES - 16, 1))
    value = 1.0 - jnp.exp(-4.0 * value)
    for channel in range(3):
        moved = pltpu.roll(value, (LANES - 32 * channel) % LANES, 1) if channel else value
        out[channel : channel + 1, :] = moved[0:1, 0:16]


def on_device(density, materials, colors, opacity):
    planes, rows, columns = density.shape
    size = lax.axis_size(AXES)
    up = [(i, i + 1) for i in range(size - 1)]
    low = lax.ppermute(density[planes - 4 :], AXES, up)
    high = lax.ppermute(density[:4], AXES, [(b, a) for a, b in up])
    any_spec = pl.BlockSpec(memory_space=pl.ANY)
    smem_spec = pl.BlockSpec(memory_space=pltpu.SMEM)
    vmem_spec = pl.BlockSpec(memory_space=pltpu.VMEM)
    partial = pl.pallas_call(
        slab_kernel,
        out_shape=jax.ShapeDtypeStruct((TILES, 8, SUBS, LANES), jnp.float32),
        in_specs=[smem_spec, smem_spec, any_spec, any_spec, any_spec, vmem_spec],
        out_specs=vmem_spec,
        scratch_shapes=[
            pltpu.VMEM((planes + 8, ROWS, LANES), jnp.float32),
            pltpu.VMEM((planes + 6, ROWS, LANES), jnp.float32),
            pltpu.VMEM((planes + 4, WIDE, LANES), jnp.float32),
            pltpu.VMEM((4, 2, 2 * planes, SUBS, LANES), jnp.float32),
            pltpu.SemaphoreType.DMA((3, TILES)),
        ],
        name="slab",
    )(colors, opacity, density, low, high, materials)
    pieces = partial.reshape(64, SUBS, LANES)
    parts = lax.all_to_all(pieces, ("x", "zl", "c"), split_axis=0, concat_axis=0, tiled=True)
    merged = pl.pallas_call(
        merge_kernel,
        out_shape=jax.ShapeDtypeStruct((16, LANES), jnp.float32),
        in_specs=[vmem_spec],
        out_specs=vmem_spec,
        name="merge",
    )(parts)
    parts = lax.all_to_all(merged, ("zh", "y"), split_axis=0, concat_axis=0, tiled=True)
    return pl.pallas_call(
        final_kernel,
        out_shape=jax.ShapeDtypeStruct((3, 16), jnp.float32),
        in_specs=[vmem_spec],
        out_specs=vmem_spec,
        name="final",
    )(parts)


def solution(mesh):
    grid = Mesh(mesh.devices.reshape(2, 8, 8, 4, 2), AXES)
    placed = (P(AXES, None, None), P(AXES, None, None), P(), P())
    return jax.shard_map(on_device, mesh=grid, in_specs=placed, out_specs=P(None, AXES), check_vma=False)
```

```python
import jax
import jax.numpy as jnp
from jax import lax
from jax.experimental import pallas as pl
from jax.experimental.pallas import tpu as pltpu
from jax.sharding import Mesh, PartitionSpec as P

LIGHT_DIR = (0.64, 0.48, 0.6)
AXES = ("zh", "y", "x", "zl", "c")
LANES, SUBS = 128, 8
PLANES = 8
TILES = 8
PITCH = 24
ROWS = PITCH * TILES + SUBS
WIDE = PITCH * (TILES + 2) + SUBS
TILE = (SUBS, LANES)
MIB = 1 << 20


def iota(axis):
    return lax.broadcasted_iota(jnp.int32, TILE, axis)


def take_lanes(values, index):
    return jnp.take_along_axis(values, index, axis=1)


def shift_columns(tiles, at, by):
    lane = iota(1)
    if by < 0:
        beside = tiles[at - 1] if at else jnp.zeros(TILE, jnp.float32)
        mixed = jnp.where(lane >= LANES + by, beside, tiles[at])
    else:
        beside = tiles[at + 1] if at + 1 < len(tiles) else jnp.zeros(TILE, jnp.float32)
        mixed = jnp.where(lane < by, beside, tiles[at])
    return pltpu.roll(mixed, (-by) % LANES, 1)


def start_row(tile, half):
    return SUBS + PITCH * tile + SUBS * half


def smooth_plane(before, here, after, target, pad, scale=None):
    near, far = 0.25, 0.125
    if scale is not None:
        near, far = near * scale, far * scale

    def at(plane, row):
        return plane[0][plane[1], pl.ds(row, SUBS), :]

    for half in range(2):
        rows = [start_row(t, half) for t in range(TILES)]
        tiles = [at(here, r) for r in rows]
        for t, r in enumerate(rows):
            beside = shift_columns(tiles, t, -1) + shift_columns(tiles, t, 1)
            beside += at(here, r - 1) + at(here, r + 1)
            beside += at(before, r) + at(after, r)
            target[0][target[1], pl.ds(r + pad, SUBS), :] = near * tiles[t] + far * beside


def clear_gaps(ref, wide):
    shape = (ref.shape[0], SUBS, LANES)
    for t in range(TILES + 1 + 2 * wide):
        ref[:, pl.ds(PITCH * t, SUBS), :] = jnp.zeros(shape, jnp.float32)
    if wide:
        for t in (0, TILES + 1):
            for half in range(2):
                ref[:, pl.ds(start_row(t, half), SUBS), :] = jnp.zeros(shape, jnp.float32)


def transposed_groups(values):
    group = iota(1) // 16
    values = list(values)
    for bit in (1, 2, 4):
        low = (group & bit) == 0
        for i in range(8):
            if not i & bit:
                a, b = values[i], values[i | bit]
                values[i] = jnp.where(low, a, pltpu.roll(b, 16 * bit, 1))
                values[i | bit] = jnp.where(low, pltpu.roll(a, LANES - 16 * bit, 1), b)
    return values


def in_plane_gradients(at):
    row = [at(0, -1), at(0, 0), at(0, 1)]
    rows_g = (at(1, 0) - at(-1, 0)) + 2.0 * (at(2, 0) - at(-2, 0))
    cols_g = (shift_columns(row, 1, 1) - shift_columns(row, 1, -1)) + 2.0 * (
        shift_columns(row, 1, 2) - shift_columns(row, 1, -2)
    )
    facing = (0.9 * LIGHT_DIR[1]) * rows_g + (0.9 * LIGHT_DIR[2]) * cols_g
    return facing, rows_g * rows_g + cols_g * cols_g + 100.0


def inner_kernel(colors, opacity, own, labels, tint, alphas, edges, once, twice, part, raw, looked):
    clear_gaps(raw, 0)
    clear_gaps(edges, 0)
    clear_gaps(once, 0)
    clear_gaps(twice, 1)
    for p in range(PLANES):
        for t in range(TILES):
            for half in range(2):
                value = own[p, pl.ds(SUBS * half, SUBS), pl.ds(LANES * t, LANES)]
                raw[p, pl.ds(start_row(t, half), SUBS), :] = value
                if p < 2 or p >= PLANES - 2:
                    edges[p % 4 if p < 2 else p - 4, pl.ds(start_row(t, half), SUBS), :] = value

    lane, sub = iota(1), iota(0)
    tables = [jnp.zeros(TILE, jnp.float32) for _ in range(4)]
    for m in range(16):
        here = lane == m
        entries = (0.5 * opacity[m], colors[0, m], colors[1, m], colors[2, m])
        tables = [jnp.where(here, e, t) for e, t in zip(entries, tables)]

    def look(p, carry):
        for half in range(2):
            for side in range(2):
                cols = slice(LANES * side, LANES * (side + 1))
                a = jnp.broadcast_to(labels[p, 2 * half : 2 * half + 1, cols], TILE)
                b = jnp.broadcast_to(labels[p, 2 * half + 1 : 2 * half + 2, cols], TILE)
                index = jnp.where(sub < 4, a, b)
                for i, table in enumerate(tables):
                    looked[i, side, 2 * p + half] = take_lanes(table, index)
        return carry

    lax.fori_loop(0, PLANES, look, 0)

    def smooth_once(k, carry):
        smooth_plane((raw, k), (raw, k + 1), (raw, k + 2), (once, k), 0)
        return carry

    def smooth_twice(k, carry):
        smooth_plane((once, k), (once, k + 1), (once, k + 2), (twice, k), PITCH)
        return carry

    lax.fori_loop(0, PLANES - 2, smooth_once, 0)
    lax.fori_loop(0, PLANES - 4, smooth_twice, 0)

    def spread_tile(t, carry):
        side = t // 4
        spread = (t % 4) * 32 + lane // 4
        start = pl.multiple_of(PITCH * t, SUBS) + PITCH
        for p in range(PLANES):
            for half in range(2):
                scale, *tints = [take_lanes(looked[i, side, 2 * p + half], spread) for i in range(4)]
                for i, value in enumerate(tints):
                    tint[i, t, 2 * p + half] = value
                if 2 <= p < PLANES - 2:

                    def at(rows, tiles):
                        return twice[p - 2, pl.ds(start + start_row(tiles, half) + rows, SUBS), :]

                    facing, length = in_plane_gradients(at)
                    part[0, t, 2 * (p - 2) + half] = facing
                    part[1, t, 2 * (p - 2) + half] = length
                    scale = scale + scale * jnp.tanh(at(0, 0))
                alphas[t, 2 * p + half] = scale
        return carry

    lax.fori_loop(0, TILES, spread_tile, 0)


def slab_kernel(low, high, tint, alphas, edges, once, twice, part, out, raw_h, once_h, twice_h, layers):
    clear_gaps(raw_h, 0)
    clear_gaps(once_h, 0)
    clear_gaps(twice_h, 1)
    for first, ref in ((0, low), (4, high)):
        for p in range(4):
            for t in range(TILES):
                for half in range(2):
                    raw_h[first + p, pl.ds(start_row(t, half), SUBS), :] = ref[
                        p, pl.ds(SUBS * half, SUBS), pl.ds(LANES * t, LANES)
                    ]

    position = lax.axis_index(AXES[0])
    total = lax.axis_size(AXES[0])
    for name in AXES[1:]:
        position = position * lax.axis_size(name) + lax.axis_index(name)
        total = total * lax.axis_size(name)
    in_front = jnp.where(position == 0, 0.0, 1.0)
    behind = jnp.where(position == total - 1, 0.0, 1.0)

    def scale(p):
        return in_front if p < 0 else behind if p >= PLANES else None

    def raw_at(p):
        if 0 <= p < PLANES:
            return edges, p if p < 4 else p - 4
        return raw_h, p + 4 if p < 0 else p - 4

    def once_at(p):
        if 1 <= p < PLANES - 1:
            return once, p - 1
        return once_h, p + 3 if p < 4 else p - 3

    def twice_at(p):
        if 2 <= p < PLANES - 2:
            return twice, p - 2
        return twice_h, p + 2 if p < 4 else p - 2

    for p in (-3, -2, -1, 0, 7, 8, 9, 10):
        smooth_plane(raw_at(p - 1), raw_at(p), raw_at(p + 1), once_at(p), 0, scale(p))
    for p in (-2, -1, 0, 1, 6, 7, 8, 9):
        smooth_plane(once_at(p - 1), once_at(p), once_at(p + 1), twice_at(p), PITCH, scale(p))

    def shade(t, carry):
        start = pl.multiple_of(PITCH * t, SUBS) + PITCH
        found = [None, None]
        for p in range(PLANES):
            for half in range(2):

                def at(planes, rows, tiles):
                    ref, index = twice_at(p + planes)
                    return ref[index, pl.ds(start + start_row(tiles, half) + rows, SUBS), :]

                alpha = alphas[t, 2 * p + half]
                if 2 <= p < PLANES - 2:
                    facing, length = (part[i, t, 2 * (p - 2) + half] for i in range(2))
                else:
                    facing, length = in_plane_gradients(lambda rows, tiles: at(0, rows, tiles))
                    alpha = alpha + alpha * jnp.tanh(at(0, 0, 0))
                depth_g = (at(1, 0, 0) - at(-1, 0, 0)) + 2.0 * (at(2, 0, 0) - at(-2, 0, 0))
                facing = facing + (0.9 * LIGHT_DIR[0]) * depth_g
                length = length + depth_g * depth_g
                light = alpha * (0.1 + jnp.abs(facing) * lax.rsqrt(length))
                tints = [tint[i, t, 2 * p + half] for i in range(3)]
                if p == 0:
                    found[half] = [c * light for c in tints] + [1.0 - alpha]
                else:
                    transmit = found[half][3]
                    light = transmit * light
                    found[half] = [a + c * light for a, c in zip(found[half], tints)] + [
                        transmit - transmit * alpha
                    ]
        for half in range(2):
            for channel in range(4):
                layers[4 * half + channel, t] = found[half][channel]
        return carry

    lax.fori_loop(0, TILES, shade, 0)

    for half in range(2):
        for channel in range(4):
            tiles = [layers[4 * half + channel, t] for t in range(TILES)]
            for g, piece in enumerate(transposed_groups(tiles)):
                out[TILES * half + g, pl.ds(SUBS * channel, SUBS), :] = piece


def merge_kernel(parts, out):
    pieces = []
    for half in range(2):
        level = [
            [parts[8 * half + s, pl.ds(SUBS * channel, SUBS), :] for channel in range(4)] for s in range(8)
        ]
        while len(level) > 1:
            level = [
                [a[i] + a[3] * b[i] for i in range(3)] + [a[3] * b[3]] for a, b in zip(level[::2], level[1::2])
            ]
        pieces += level[0][:3] + [1.0 - level[0][3]]
    for g, piece in enumerate(transposed_groups(pieces)):
        out[pl.ds(g, SUBS, stride=SUBS), :] = piece


def final_kernel(parts, out):
    lane = iota(1)
    cover = (lane & 64) + 48 + lane % 16

    def over(front, back):
        return front + (1.0 - take_lanes(front, cover)) * back

    level = [parts[pl.ds(j, SUBS, stride=SUBS), :] for j in range(8)]
    while len(level) > 1:
        level = [over(a, b) for a, b in zip(level[::2], level[1::2])]
    value = level[0]
    for step in (1, 2, 4):
        value = over(value, pltpu.roll(value, SUBS - step, 0))
    value = over(value, pltpu.roll(value, 64, 1))
    value = 1.0 - jnp.exp(-4.0 * value)
    for channel in range(3):
        moved = pltpu.roll(value, LANES - 16 * channel, 1) if channel else value
        out[channel : channel + 1, :] = moved[0:1, 0:16]


VMEM_SPEC = pl.BlockSpec(memory_space=pltpu.VMEM)
SMEM_SPEC = pl.BlockSpec(memory_space=pltpu.SMEM)
INNER_OUT = (
    (3, TILES, 2 * PLANES, SUBS, LANES),
    (TILES, 2 * PLANES, SUBS, LANES),
    (4, ROWS, LANES),
    (PLANES - 2, ROWS, LANES),
    (PLANES - 4, WIDE, LANES),
    (2, TILES, 2 * (PLANES - 4), SUBS, LANES),
)
INNER_SCRATCH = ((PLANES, ROWS, LANES), (4, 2, 2 * PLANES, SUBS, LANES))
SLAB_SCRATCH = ((8, ROWS, LANES), (8, ROWS, LANES), (8, WIDE, LANES), (8, TILES, SUBS, LANES))


def run(kernel, shapes, scratch, in_specs, limit, name, cost=None):
    return pl.pallas_call(
        kernel,
        out_shape=[jax.ShapeDtypeStruct(s, jnp.float32) for s in shapes],
        in_specs=in_specs,
        out_specs=[VMEM_SPEC] * len(shapes),
        scratch_shapes=[pltpu.VMEM(s, jnp.float32) for s in scratch],
        compiler_params=pltpu.CompilerParams(vmem_limit_bytes=limit * MIB),
        cost_estimate=cost,
        name=name,
    )


def render(low, high, density, materials, colors, opacity):
    cost = pl.CostEstimate(flops=20_000_000, bytes_accessed=8_000_000, transcendentals=100_000)
    inner = run(inner_kernel, INNER_OUT, INNER_SCRATCH, [SMEM_SPEC] * 2 + [VMEM_SPEC] * 2, 16, "inner", cost)(
        colors, opacity, density, materials
    )
    return run(slab_kernel, [(16, 32, LANES)], SLAB_SCRATCH, [VMEM_SPEC] * 8, 16, "slab")(low, high, *inner)[0]


def on_device(density, materials, colors, opacity):
    size = lax.axis_size(AXES)
    up = [(i, i + 1) for i in range(size - 1)]
    low = lax.ppermute(density[PLANES - 4 :], AXES, up)
    high = lax.ppermute(density[:4], AXES, [(b, a) for a, b in up])
    pieces = render(low, high, density, materials, colors, opacity)
    parts = lax.all_to_all(pieces, ("zh", "zl", "c"), split_axis=0, concat_axis=0, tiled=True)
    rows = run(merge_kernel, [(64, LANES)], (), [VMEM_SPEC], 2, "merge")(parts)[0]
    rows = lax.all_to_all(rows, ("y", "x"), split_axis=0, concat_axis=0, tiled=True)
    return run(final_kernel, [(3, 16)], (), [VMEM_SPEC], 2, "final")(rows)[0]


def solution(mesh):
    grid = Mesh(mesh.devices.reshape(2, 8, 8, 4, 2), AXES)
    placed = (P(AXES, None, None), P(AXES, None, None), P(), P())
    return jax.shard_map(on_device, mesh=grid, in_specs=placed, out_specs=P(None, AXES), check_vma=False)
```

```python
import jax
import jax.numpy as jnp
from jax import lax
from jax.experimental import pallas as pl
from jax.experimental.pallas import tpu as pltpu
from jax.sharding import Mesh, PartitionSpec as P

LIGHT_DIR = (0.64, 0.48, 0.6)
AXES = ("zh", "y", "x", "zl", "c")
LANES, SUBS = 128, 8
PLANES = 8
TILES = 8
PITCH = 24
ROWS = PITCH * TILES + SUBS
WIDE = PITCH * (TILES + 2) + SUBS
TILE = (SUBS, LANES)
MIB = 1 << 20


def iota(axis):
    return lax.broadcasted_iota(jnp.int32, TILE, axis)


def take_lanes(values, index):
    return jnp.take_along_axis(values, index, axis=1)


def shift_columns(tiles, at, by):
    lane = iota(1)
    if by < 0:
        beside = tiles[at - 1] if at else jnp.zeros(TILE, jnp.float32)
        mixed = jnp.where(lane >= LANES + by, beside, tiles[at])
    else:
        beside = tiles[at + 1] if at + 1 < len(tiles) else jnp.zeros(TILE, jnp.float32)
        mixed = jnp.where(lane < by, beside, tiles[at])
    return pltpu.roll(mixed, (-by) % LANES, 1)


def start_row(tile, half):
    return SUBS + PITCH * tile + SUBS * half


def smooth_plane(before, here, after, target, pad, scale=None):
    near, far = 0.25, 0.125
    if scale is not None:
        near, far = near * scale, far * scale

    def at(plane, row):
        return plane[0][plane[1], pl.ds(row, SUBS), :]

    for half in range(2):
        rows = [start_row(t, half) for t in range(TILES)]
        tiles = [at(here, r) for r in rows]
        for t, r in enumerate(rows):
            beside = shift_columns(tiles, t, -1) + shift_columns(tiles, t, 1)
            beside += at(here, r - 1) + at(here, r + 1)
            beside += at(before, r) + at(after, r)
            target[0][target[1], pl.ds(r + pad, SUBS), :] = near * tiles[t] + far * beside


def clear_gaps(ref, wide):
    shape = (ref.shape[0], SUBS, LANES)
    for t in range(TILES + 1 + 2 * wide):
        ref[:, pl.ds(PITCH * t, SUBS), :] = jnp.zeros(shape, jnp.float32)
    if wide:
        for t in (0, TILES + 1):
            for half in range(2):
                ref[:, pl.ds(start_row(t, half), SUBS), :] = jnp.zeros(shape, jnp.float32)


def transposed_groups(values):
    group = iota(1) // 16
    values = list(values)
    for bit in (1, 2, 4):
        low = (group & bit) == 0
        for i in range(8):
            if not i & bit:
                a, b = values[i], values[i | bit]
                values[i] = jnp.where(low, a, pltpu.roll(b, 16 * bit, 1))
                values[i | bit] = jnp.where(low, pltpu.roll(a, LANES - 16 * bit, 1), b)
    return values


def in_plane_gradients(at):
    row = [at(0, -1), at(0, 0), at(0, 1)]
    rows_g = (at(1, 0) - at(-1, 0)) + 2.0 * (at(2, 0) - at(-2, 0))
    cols_g = (shift_columns(row, 1, 1) - shift_columns(row, 1, -1)) + 2.0 * (
        shift_columns(row, 1, 2) - shift_columns(row, 1, -2)
    )
    facing = (0.9 * LIGHT_DIR[1]) * rows_g + (0.9 * LIGHT_DIR[2]) * cols_g
    return facing, rows_g * rows_g + cols_g * cols_g + 100.0


def fetch_kernel(density, materials, far, near, own, labels, sems):
    back = 4 * lax.axis_index("c")
    copies = [
        pltpu.make_async_copy(density.at[pl.ds(back, 4)], far, sems.at[0]),
        pltpu.make_async_copy(density.at[pl.ds(4 - back, 4)], near, sems.at[1]),
        pltpu.make_async_copy(density, own, sems.at[2]),
        pltpu.make_async_copy(materials, labels, sems.at[3]),
    ]
    for copy in copies:
        copy.start()
    for copy in copies:
        copy.wait()


def inner_kernel(colors_hbm, opacity_hbm, own, labels, tint, alphas, edges, once, twice, part, raw, looked, colors, opacity, sems):
    copies = [
        pltpu.make_async_copy(colors_hbm, colors, sems.at[0]),
        pltpu.make_async_copy(opacity_hbm, opacity, sems.at[1]),
    ]
    for copy in copies:
        copy.start()
    clear_gaps(raw, 0)
    clear_gaps(edges, 0)
    clear_gaps(once, 0)
    clear_gaps(twice, 1)
    for p in range(PLANES):
        for t in range(TILES):
            for half in range(2):
                value = own[p, pl.ds(SUBS * half, SUBS), pl.ds(LANES * t, LANES)]
                raw[p, pl.ds(start_row(t, half), SUBS), :] = value
                if p < 2 or p >= PLANES - 2:
                    edges[p % 4 if p < 2 else p - 4, pl.ds(start_row(t, half), SUBS), :] = value

    for copy in copies:
        copy.wait()
    lane, sub = iota(1), iota(0)
    tables = [jnp.zeros(TILE, jnp.float32) for _ in range(4)]
    for m in range(16):
        here = lane == m
        entries = (0.5 * opacity[m], colors[0, m], colors[1, m], colors[2, m])
        tables = [jnp.where(here, e, t) for e, t in zip(entries, tables)]

    def look(p, carry):
        for half in range(2):
            for side in range(2):
                cols = slice(LANES * side, LANES * (side + 1))
                a = jnp.broadcast_to(labels[p, 2 * half : 2 * half + 1, cols], TILE)
                b = jnp.broadcast_to(labels[p, 2 * half + 1 : 2 * half + 2, cols], TILE)
                index = jnp.where(sub < 4, a, b)
                for i, table in enumerate(tables):
                    looked[i, side, 2 * p + half] = take_lanes(table, index)
        return carry

    lax.fori_loop(0, PLANES, look, 0)

    def smooth_once(k, carry):
        smooth_plane((raw, k), (raw, k + 1), (raw, k + 2), (once, k), 0)
        return carry

    def smooth_twice(k, carry):
        smooth_plane((once, k), (once, k + 1), (once, k + 2), (twice, k), PITCH)
        return carry

    lax.fori_loop(0, PLANES - 2, smooth_once, 0)
    lax.fori_loop(0, PLANES - 4, smooth_twice, 0)

    def spread_tile(t, carry):
        side = t // 4
        spread = (t % 4) * 32 + lane // 4
        start = pl.multiple_of(PITCH * t, SUBS) + PITCH
        for p in range(PLANES):
            for half in range(2):
                scale, *tints = [take_lanes(looked[i, side, 2 * p + half], spread) for i in range(4)]
                for i, value in enumerate(tints):
                    tint[i, t, 2 * p + half] = value
                if 2 <= p < PLANES - 2:

                    def at(rows, tiles):
                        return twice[p - 2, pl.ds(start + start_row(tiles, half) + rows, SUBS), :]

                    facing, length = in_plane_gradients(at)
                    part[0, t, 2 * (p - 2) + half] = facing
                    part[1, t, 2 * (p - 2) + half] = length
                    scale = scale + scale * jnp.tanh(at(0, 0))
                alphas[t, 2 * p + half] = scale
        return carry

    lax.fori_loop(0, TILES, spread_tile, 0)


def slab_kernel(far, near, tint, alphas, edges, once, twice, part, out, raw_h, once_h, twice_h, layers):
    clear_gaps(raw_h, 0)
    clear_gaps(once_h, 0)
    clear_gaps(twice_h, 1)
    back = 4 * lax.axis_index("c")
    for first, ref in ((back, far), (4 - back, near)):
        for p in range(4):
            for t in range(TILES):
                for half in range(2):
                    raw_h[first + p, pl.ds(start_row(t, half), SUBS), :] = ref[
                        p, pl.ds(SUBS * half, SUBS), pl.ds(LANES * t, LANES)
                    ]

    position = lax.axis_index(AXES[0])
    total = lax.axis_size(AXES[0])
    for name in AXES[1:]:
        position = position * lax.axis_size(name) + lax.axis_index(name)
        total = total * lax.axis_size(name)
    in_front = jnp.where(position == 0, 0.0, 1.0)
    behind = jnp.where(position == total - 1, 0.0, 1.0)

    def scale(p):
        return in_front if p < 0 else behind if p >= PLANES else None

    def raw_at(p):
        if 0 <= p < PLANES:
            return edges, p if p < 4 else p - 4
        return raw_h, p + 4 if p < 0 else p - 4

    def once_at(p):
        if 1 <= p < PLANES - 1:
            return once, p - 1
        return once_h, p + 3 if p < 4 else p - 3

    def twice_at(p):
        if 2 <= p < PLANES - 2:
            return twice, p - 2
        return twice_h, p + 2 if p < 4 else p - 2

    for p in (-3, -2, -1, 0, 7, 8, 9, 10):
        smooth_plane(raw_at(p - 1), raw_at(p), raw_at(p + 1), once_at(p), 0, scale(p))
    for p in (-2, -1, 0, 1, 6, 7, 8, 9):
        smooth_plane(once_at(p - 1), once_at(p), once_at(p + 1), twice_at(p), PITCH, scale(p))

    def shade(t, carry):
        start = pl.multiple_of(PITCH * t, SUBS) + PITCH
        found = [None, None]
        for p in range(PLANES):
            for half in range(2):

                def at(planes, rows, tiles):
                    ref, index = twice_at(p + planes)
                    return ref[index, pl.ds(start + start_row(tiles, half) + rows, SUBS), :]

                alpha = alphas[t, 2 * p + half]
                if 2 <= p < PLANES - 2:
                    facing, length = (part[i, t, 2 * (p - 2) + half] for i in range(2))
                else:
                    facing, length = in_plane_gradients(lambda rows, tiles: at(0, rows, tiles))
                    alpha = alpha + alpha * jnp.tanh(at(0, 0, 0))
                depth_g = (at(1, 0, 0) - at(-1, 0, 0)) + 2.0 * (at(2, 0, 0) - at(-2, 0, 0))
                facing = facing + (0.9 * LIGHT_DIR[0]) * depth_g
                length = length + depth_g * depth_g
                light = alpha * (0.1 + jnp.abs(facing) * lax.rsqrt(length))
                tints = [tint[i, t, 2 * p + half] for i in range(3)]
                if p == 0:
                    found[half] = [c * light for c in tints] + [1.0 - alpha]
                else:
                    transmit = found[half][3]
                    light = transmit * light
                    found[half] = [a + c * light for a, c in zip(found[half], tints)] + [
                        transmit - transmit * alpha
                    ]
        for half in range(2):
            for channel in range(4):
                layers[4 * half + channel, t] = found[half][channel]
        return carry

    lax.fori_loop(0, TILES, shade, 0)

    for half in range(2):
        for channel in range(4):
            tiles = [layers[4 * half + channel, t] for t in range(TILES)]
            for g, piece in enumerate(transposed_groups(tiles)):
                out[TILES * half + g, pl.ds(SUBS * channel, SUBS), :] = piece


def merge_kernel(parts, out):
    pieces = []
    for half in range(2):
        level = [
            [parts[8 * half + s, pl.ds(SUBS * channel, SUBS), :] for channel in range(4)] for s in range(8)
        ]
        while len(level) > 1:
            level = [
                [a[i] + a[3] * b[i] for i in range(3)] + [a[3] * b[3]] for a, b in zip(level[::2], level[1::2])
            ]
        pieces += level[0][:3] + [1.0 - level[0][3]]
    for g, piece in enumerate(transposed_groups(pieces)):
        out[pl.ds(g, SUBS, stride=SUBS), :] = piece


def final_kernel(parts, out):
    lane = iota(1)
    cover = (lane & 64) + 48 + lane % 16

    def over(front, back):
        return front + (1.0 - take_lanes(front, cover)) * back

    level = [parts[pl.ds(j, SUBS, stride=SUBS), :] for j in range(8)]
    while len(level) > 1:
        level = [over(a, b) for a, b in zip(level[::2], level[1::2])]
    value = level[0]
    for step in (1, 2, 4):
        value = over(value, pltpu.roll(value, SUBS - step, 0))
    value = over(value, pltpu.roll(value, 64, 1))
    value = 1.0 - jnp.exp(-4.0 * value)
    for channel in range(3):
        moved = pltpu.roll(value, LANES - 16 * channel, 1) if channel else value
        out[channel : channel + 1, :] = moved[0:1, 0:16]


VMEM_SPEC = pl.BlockSpec(memory_space=pltpu.VMEM)
HBM_SPEC = pl.BlockSpec(memory_space=pltpu.HBM)
INNER_OUT = (
    (3, TILES, 2 * PLANES, SUBS, LANES),
    (TILES, 2 * PLANES, SUBS, LANES),
    (4, ROWS, LANES),
    (PLANES - 2, ROWS, LANES),
    (PLANES - 4, WIDE, LANES),
    (2, TILES, 2 * (PLANES - 4), SUBS, LANES),
)
INNER_SCRATCH = ((PLANES, ROWS, LANES), (4, 2, 2 * PLANES, SUBS, LANES))
SLAB_SCRATCH = ((8, ROWS, LANES), (8, ROWS, LANES), (8, WIDE, LANES), (8, TILES, SUBS, LANES))


def run(kernel, shapes, scratch, in_specs, limit, name, cost=None):
    return pl.pallas_call(
        kernel,
        out_shape=[jax.ShapeDtypeStruct(s, d) for s, d in shapes],
        in_specs=in_specs,
        out_specs=[VMEM_SPEC] * len(shapes),
        scratch_shapes=scratch,
        compiler_params=pltpu.CompilerParams(vmem_limit_bytes=limit * MIB),
        cost_estimate=cost,
        name=name,
    )


def floats(*shapes):
    return [(s, jnp.float32) for s in shapes]


def vmem(*shapes):
    return [pltpu.VMEM(s, jnp.float32) for s in shapes]


def fetch(density, materials):
    edge = (4,) + density.shape[1:]
    shapes = floats(edge, edge, density.shape) + [(materials.shape, materials.dtype)]
    return run(fetch_kernel, shapes, [pltpu.SemaphoreType.DMA((4,))], [HBM_SPEC] * 2, 4, "fetch")(density, materials)


def render_inner(density, materials, colors, opacity):
    cost = pl.CostEstimate(flops=20_000_000, bytes_accessed=8_000_000, transcendentals=100_000)
    scratch = vmem(*INNER_SCRATCH) + [
        pltpu.SMEM(colors.shape, jnp.float32),
        pltpu.SMEM(opacity.shape, jnp.float32),
        pltpu.SemaphoreType.DMA((2,)),
    ]
    specs = [HBM_SPEC] * 2 + [VMEM_SPEC] * 2
    return run(inner_kernel, floats(*INNER_OUT), scratch, specs, 16, "inner", cost)(
        colors, opacity, density, materials
    )


def render(far, near, inner):
    return run(slab_kernel, floats((16, 32, LANES)), vmem(*SLAB_SCRATCH), [VMEM_SPEC] * 8, 16, "slab")(
        far, near, *inner
    )[0]


def on_device(density, materials, colors, opacity):
    size = lax.axis_size(AXES)
    beside = [(i, i ^ 1) for i in range(size)]
    across = [(i, i + 1) for i in range(1, size - 1, 2)]
    across += [(b, a) for a, b in across]
    density, materials, colors, opacity = (
        pltpu.with_memory_space_constraint(a, pltpu.HBM) for a in (density, materials, colors, opacity)
    )
    far, near, density, materials = fetch(density, materials)
    far = lax.ppermute(far, AXES, across)
    near = lax.ppermute(near, AXES, beside)
    pieces = render(far, near, render_inner(density, materials, colors, opacity))
    parts = lax.all_to_all(pieces, ("zh", "zl", "c"), split_axis=0, concat_axis=0, tiled=True)
    rows = run(merge_kernel, floats((64, LANES)), (), [VMEM_SPEC], 2, "merge")(parts)[0]
    rows = lax.all_to_all(rows, ("y", "x"), split_axis=0, concat_axis=0, tiled=True)
    return run(final_kernel, floats((3, 16)), (), [VMEM_SPEC], 2, "final")(rows)[0]


def solution(mesh):
    grid = Mesh(mesh.devices.reshape(2, 8, 8, 4, 2), AXES)
    placed = (P(AXES, None, None), P(AXES, None, None), P(), P())
    return jax.shard_map(on_device, mesh=grid, in_specs=placed, out_specs=P(None, AXES), check_vma=False)
```

```python
import jax
import jax.numpy as jnp
from jax import lax
from jax.experimental import pallas as pl
from jax.experimental.pallas import tpu as pltpu
from jax.sharding import Mesh, PartitionSpec as P


LIGHT_DIR = (0.64, 0.48, 0.6)
AXES = ("zh", "y", "x", "zl", "c")
LANES, SUBS = 128, 8
PLANES = 8
TILES = 8
PITCH = 24
ROWS = PITCH * TILES + SUBS
WIDE = PITCH * (TILES + 2) + SUBS
TILE = (SUBS, LANES)
MIB = 1 << 20


def iota(axis):
    return lax.broadcasted_iota(jnp.int32, TILE, axis)


def take_lanes(values, index):
    return jnp.take_along_axis(values, index, axis=1)


def shift_columns(tiles, at, by):
    lane = iota(1)
    if by < 0:
        beside = tiles[at - 1] if at else jnp.zeros(TILE, jnp.float32)
        mixed = jnp.where(lane >= LANES + by, beside, tiles[at])
    else:
        beside = tiles[at + 1] if at + 1 < len(tiles) else jnp.zeros(TILE, jnp.float32)
        mixed = jnp.where(lane < by, beside, tiles[at])
    return pltpu.roll(mixed, (-by) % LANES, 1)


def start_row(tile, half):
    return SUBS + PITCH * tile + SUBS * half


def smooth_plane(before, here, after, target, pad, scale=None):
    near, far = 0.25, 0.125
    if scale is not None:
        near, far = near * scale, far * scale

    def at(plane, row):
        return plane[0][plane[1], pl.ds(row, SUBS), :]

    for half in range(2):
        rows = [start_row(t, half) for t in range(TILES)]
        tiles = [at(here, r) for r in rows]
        for t, r in enumerate(rows):
            beside = shift_columns(tiles, t, -1) + shift_columns(tiles, t, 1)
            beside += at(here, r - 1) + at(here, r + 1)
            beside += at(before, r) + at(after, r)
            target[0][target[1], pl.ds(r + pad, SUBS), :] = near * tiles[t] + far * beside


def clear_gaps(ref, wide):
    shape = (ref.shape[0], SUBS, LANES)
    for t in range(TILES + 1 + 2 * wide):
        ref[:, pl.ds(PITCH * t, SUBS), :] = jnp.zeros(shape, jnp.float32)
    if wide:
        for t in (0, TILES + 1):
            for half in range(2):
                ref[:, pl.ds(start_row(t, half), SUBS), :] = jnp.zeros(shape, jnp.float32)


def transposed_groups(values):
    group = iota(1) // 16
    values = list(values)
    for bit in (1, 2, 4):
        low = (group & bit) == 0
        for i in range(8):
            if not i & bit:
                a, b = values[i], values[i | bit]
                values[i] = jnp.where(low, a, pltpu.roll(b, 16 * bit, 1))
                values[i | bit] = jnp.where(low, pltpu.roll(a, LANES - 16 * bit, 1), b)
    return values


def in_plane_gradients(at):
    row = [at(0, -1), at(0, 0), at(0, 1)]
    rows_g = (at(1, 0) - at(-1, 0)) + 2.0 * (at(2, 0) - at(-2, 0))
    cols_g = (shift_columns(row, 1, 1) - shift_columns(row, 1, -1)) + 2.0 * (
        shift_columns(row, 1, 2) - shift_columns(row, 1, -2)
    )
    facing = (0.9 * LIGHT_DIR[1]) * rows_g + (0.9 * LIGHT_DIR[2]) * cols_g
    return facing, rows_g * rows_g + cols_g * cols_g + 100.0


def fetch_kernel(density, materials, far, near, labels, sems):
    back = 4 * lax.axis_index("c")
    copies = [
        pltpu.make_async_copy(density.at[pl.ds(back, 4)], far, sems.at[0]),
        pltpu.make_async_copy(density.at[pl.ds(4 - back, 4)], near, sems.at[1]),
        pltpu.make_async_copy(materials, labels, sems.at[2]),
    ]
    for copy in copies:
        copy.start()
    for copy in copies:
        copy.wait()


def spread_planes(source, target, place):
    for p in range(4):
        for t in range(TILES):
            for half in range(2):
                target[place(p), pl.ds(start_row(t, half), SUBS), :] = source[
                    p, pl.ds(SUBS * half, SUBS), pl.ds(LANES * t, LANES)
                ]


def inner_kernel(
    colors_hbm, opacity_hbm, far, near, labels, tint, alphas, raw, once, twice, part, looked, colors, opacity, sems
):
    copies = [
        pltpu.make_async_copy(colors_hbm, colors, sems.at[0]),
        pltpu.make_async_copy(opacity_hbm, opacity, sems.at[1]),
    ]
    for copy in copies:
        copy.start()
    clear_gaps(raw, 0)
    clear_gaps(once, 0)
    clear_gaps(twice, 1)
    back = 4 * lax.axis_index("c")
    spread_planes(far, raw, lambda p: back + p)
    spread_planes(near, raw, lambda p: 4 - back + p)

    for copy in copies:
        copy.wait()
    lane, sub = iota(1), iota(0)
    tables = [jnp.zeros(TILE, jnp.float32) for _ in range(4)]
    for m in range(16):
        here = lane == m
        entries = (0.5 * opacity[m], colors[0, m], colors[1, m], colors[2, m])
        tables = [jnp.where(here, e, t) for e, t in zip(entries, tables)]

    def look(p, carry):
        for half in range(2):
            for side in range(2):
                cols = slice(LANES * side, LANES * (side + 1))
                a = jnp.broadcast_to(labels[p, 2 * half : 2 * half + 1, cols], TILE)
                b = jnp.broadcast_to(labels[p, 2 * half + 1 : 2 * half + 2, cols], TILE)
                index = jnp.where(sub < 4, a, b)
                for i, table in enumerate(tables):
                    looked[i, side, 2 * p + half] = take_lanes(table, index)
        return carry

    lax.fori_loop(0, PLANES, look, 0)

    def smooth_once(p, carry):
        smooth_plane((raw, p - 1), (raw, p), (raw, p + 1), (once, p - 1), 0)
        return carry

    def smooth_twice(p, carry):
        smooth_plane((once, p - 2), (once, p - 1), (once, p), (twice, p - 2), PITCH)
        return carry

    lax.fori_loop(1, PLANES - 1, smooth_once, 0)
    lax.fori_loop(2, PLANES - 2, smooth_twice, 0)

    def spread_tile(t, carry):
        side = t // 4
        spread = (t % 4) * 32 + lane // 4
        start = pl.multiple_of(PITCH * t, SUBS) + PITCH
        for p in range(PLANES):
            for half in range(2):
                scale, *tints = [take_lanes(looked[i, side, 2 * p + half], spread) for i in range(4)]
                for i, value in enumerate(tints):
                    tint[i, t, 2 * p + half] = value
                if 2 <= p < PLANES - 2:

                    def at(rows, tiles):
                        return twice[p - 2, pl.ds(start + start_row(tiles, half) + rows, SUBS), :]

                    facing, length = in_plane_gradients(at)
                    part[0, t, 2 * p + half] = facing
                    part[1, t, 2 * p + half] = length
                    scale = scale + scale * jnp.tanh(at(0, 0))
                alphas[t, 2 * p + half] = scale
        return carry

    lax.fori_loop(0, TILES, spread_tile, 0)


def render_half(side, beyond, tint, alphas, raw, once, twice, part, raw_h, once_h, twice_h, shades):
    clear_gaps(raw_h, 0)
    clear_gaps(once_h, 0)
    clear_gaps(twice_h, 1)
    spread_planes(beyond, raw_h, lambda p: jnp.where(side == 0, 3 - p, p))
    position = lax.axis_index(AXES[0])
    total = lax.axis_size(AXES[0])
    for name in AXES[1:]:
        position = position * lax.axis_size(name) + lax.axis_index(name)
        total = total * lax.axis_size(name)
    outside = jnp.where(position == side * (total - 1), 0.0, 1.0)
    step = 1 - 2 * side

    def plane(j):
        return side * (PLANES - 1) + step * j

    def raw_at(j):
        return (raw, plane(j)) if j >= 0 else (raw_h, -1 - j)

    def once_at(j):
        return (once, plane(j) - 1) if j >= 1 else (once_h, -j)

    def twice_at(j):
        return (twice, plane(j) - 2) if j >= 2 else (twice_h, 1 - j)

    for j in (-3, -2, -1, 0):
        smooth_plane(raw_at(j - 1), raw_at(j), raw_at(j + 1), once_at(j), 0, outside if j < 0 else None)
    for j in (-2, -1, 0, 1):
        smooth_plane(once_at(j - 1), once_at(j), once_at(j + 1), twice_at(j), PITCH, outside if j < 0 else None)
    depth_weight = (0.9 * LIGHT_DIR[0]) * step.astype(jnp.float32)

    def shade(t):
        start = pl.multiple_of(PITCH * t, SUBS) + PITCH
        for j in range(4):
            p = plane(j)
            for half in range(2):

                def at(planes, rows, tiles):
                    ref, index = twice_at(j + planes)
                    return ref[index, pl.ds(start + start_row(tiles, half) + rows, SUBS), :]

                alpha = alphas[t, 2 * p + half]
                if j >= 2:
                    facing, length = (part[i, t, 2 * p + half] for i in range(2))
                else:
                    facing, length = in_plane_gradients(lambda rows, tiles: at(0, rows, tiles))
                    alpha = alpha + alpha * jnp.tanh(at(0, 0, 0))
                depth_g = (at(1, 0, 0) - at(-1, 0, 0)) + 2.0 * (at(2, 0, 0) - at(-2, 0, 0))
                facing = facing + depth_weight * depth_g
                length = length + depth_g * depth_g
                k = p - 4 * side
                shades[2 * half, k] = alpha
                shades[2 * half + 1, k] = alpha * (0.1 + jnp.abs(facing) * lax.rsqrt(length))
        found = []
        for half in range(2):
            for k in range(4):
                alpha, light = shades[2 * half, k], shades[2 * half + 1, k]
                tints = [tint[i, t, 2 * (k + 4 * side) + half] for i in range(3)]
                if k == 0:
                    layer = [c * light for c in tints] + [1.0 - alpha]
                else:
                    transmit = layer[3]
                    light = transmit * light
                    layer = [a + c * light for a, c in zip(layer, tints)] + [transmit - transmit * alpha]
            found.append(layer)
        return found

    return shade


def near_kernel(beyond, tint, alphas, raw, once, twice, part, layers, *scratch):
    shade = render_half(1 - lax.axis_index("c"), beyond, tint, alphas, raw, once, twice, part, *scratch)

    def body(t, carry):
        for half, layer in enumerate(shade(t)):
            for channel, value in enumerate(layer):
                layers[4 * half + channel, t] = value
        return carry

    lax.fori_loop(0, TILES, body, 0)


def far_kernel(beyond, tint, alphas, raw, once, twice, part, others, out, layers, *scratch):
    side = lax.axis_index("c")
    shade = render_half(side, beyond, tint, alphas, raw, once, twice, part, *scratch)

    def body(t, carry):
        for half, layer in enumerate(shade(t)):
            other = [others[4 * half + channel, t] for channel in range(4)]
            front = [jnp.where(side == 0, a, b) for a, b in zip(layer, other)]
            back = [jnp.where(side == 0, b, a) for a, b in zip(layer, other)]
            for channel in range(4):
                value = front[3] * back[channel]
                layers[4 * half + channel, t] = value if channel == 3 else front[channel] + value
        return carry

    lax.fori_loop(0, TILES, body, 0)
    for half in range(2):
        for channel in range(4):
            tiles = [layers[4 * half + channel, t] for t in range(TILES)]
            for g, piece in enumerate(transposed_groups(tiles)):
                out[TILES * half + g, pl.ds(SUBS * channel, SUBS), :] = piece


def merge_kernel(parts, out):
    pieces = []
    for half in range(2):
        level = [
            [parts[8 * half + s, pl.ds(SUBS * channel, SUBS), :] for channel in range(4)] for s in range(8)
        ]
        while len(level) > 1:
            level = [
                [a[i] + a[3] * b[i] for i in range(3)] + [a[3] * b[3]] for a, b in zip(level[::2], level[1::2])
            ]
        pieces += level[0][:3] + [1.0 - level[0][3]]
    for g, piece in enumerate(transposed_groups(pieces)):
        out[pl.ds(g, SUBS, stride=SUBS), :] = piece


def final_kernel(parts, out):
    lane = iota(1)
    cover = (lane & 64) + 48 + lane % 16

    def over(front, back):
        return front + (1.0 - take_lanes(front, cover)) * back

    level = [parts[pl.ds(j, SUBS, stride=SUBS), :] for j in range(8)]
    while len(level) > 1:
        level = [over(a, b) for a, b in zip(level[::2], level[1::2])]
    value = level[0]
    for step in (1, 2, 4):
        value = over(value, pltpu.roll(value, SUBS - step, 0))
    value = over(value, pltpu.roll(value, 64, 1))
    value = 1.0 - jnp.exp(-4.0 * value)
    for channel in range(3):
        moved = pltpu.roll(value, LANES - 16 * channel, 1) if channel else value
        out[channel : channel + 1, :] = moved[0:1, 0:16]


VMEM_SPEC = pl.BlockSpec(memory_space=pltpu.VMEM)
HBM_SPEC = pl.BlockSpec(memory_space=pltpu.HBM)
RAW, ONCE, TWICE = (PLANES, ROWS, LANES), (PLANES - 2, ROWS, LANES), (PLANES - 4, WIDE, LANES)
SHADED = (TILES, 2 * PLANES, SUBS, LANES)
LAYERS = (8, TILES, SUBS, LANES)
HALF = ((4, ROWS, LANES), (4, ROWS, LANES), (4, WIDE, LANES), (4, 4, SUBS, LANES))


def run(kernel, shapes, scratch, in_specs, limit, cost=None):
    return pl.pallas_call(
        kernel,
        out_shape=[jax.ShapeDtypeStruct(s, d) for s, d in shapes],
        in_specs=in_specs,
        out_specs=[VMEM_SPEC] * len(shapes),
        scratch_shapes=scratch,
        compiler_params=pltpu.CompilerParams(vmem_limit_bytes=limit * MIB),
        cost_estimate=cost,
    )


def floats(*shapes):
    return [(s, jnp.float32) for s in shapes]


def vmem(*shapes):
    return [pltpu.VMEM(s, jnp.float32) for s in shapes]


def fetch(density, materials):
    edge = (4,) + density.shape[1:]
    shapes = floats(edge, edge) + [(materials.shape, materials.dtype)]
    return run(fetch_kernel, shapes, [pltpu.SemaphoreType.DMA((3,))], [HBM_SPEC] * 2, 4)(density, materials)


def render_inner(far, near, labels, colors, opacity):
    cost = pl.CostEstimate(flops=20_000_000, bytes_accessed=8_000_000, transcendentals=100_000)
    scratch = vmem((4, 2, 2 * PLANES, SUBS, LANES)) + [
        pltpu.SMEM(colors.shape, jnp.float32),
        pltpu.SMEM(opacity.shape, jnp.float32),
        pltpu.SemaphoreType.DMA((2,)),
    ]
    specs = [HBM_SPEC] * 2 + [VMEM_SPEC] * 3
    shapes = floats((3,) + SHADED, SHADED, RAW, ONCE, TWICE, (2,) + SHADED)
    return run(inner_kernel, shapes, scratch, specs, 16, cost)(colors, opacity, far, near, labels)


def render(far, near, inner):
    cost = pl.CostEstimate(flops=5_000_000, bytes_accessed=4_000_000, transcendentals=50_000)
    layers = run(near_kernel, floats(LAYERS), vmem(*HALF), [VMEM_SPEC] * 7, 16, cost)(near, *inner)
    pieces = floats((16, 32, LANES))
    return run(far_kernel, pieces, vmem(LAYERS, *HALF), [VMEM_SPEC] * 8, 16)(far, *inner, layers[0])[0]


def on_device(density, materials, colors, opacity):
    size = lax.axis_size(AXES)
    beside = [(i, i ^ 1) for i in range(size)]
    across = [(i, i + 1) for i in range(1, size - 1, 2)]
    across += [(b, a) for a, b in across]
    density, materials, colors, opacity = (
        pltpu.with_memory_space_constraint(a, pltpu.HBM) for a in (density, materials, colors, opacity)
    )
    far, near, labels = fetch(density, materials)
    inner = render_inner(far, near, labels, colors, opacity)
    far = lax.ppermute(far, AXES, across)
    near = lax.ppermute(near, AXES, beside)
    pieces = render(far, near, inner)
    parts = lax.all_to_all(pieces, ("zh", "zl", "c"), split_axis=0, concat_axis=0, tiled=True)
    rows = run(merge_kernel, floats((64, LANES)), (), [VMEM_SPEC], 2)(parts)[0]
    rows = lax.all_to_all(rows, ("y", "x"), split_axis=0, concat_axis=0, tiled=True)
    return run(final_kernel, floats((3, 16)), (), [VMEM_SPEC], 2)(rows)[0]


def solution(mesh):
    grid = Mesh(mesh.devices.reshape(2, 8, 8, 4, 2), AXES)
    placed = (P(AXES, None, None), P(AXES, None, None), P(), P())
    return jax.shard_map(on_device, mesh=grid, in_specs=placed, out_specs=P(None, AXES), check_vma=False)
```

```python
import jax
import jax.numpy as jnp
from jax import lax
from jax.experimental import pallas as pl
from jax.experimental.pallas import tpu as pltpu
from jax.sharding import Mesh, PartitionSpec as P


LIGHT_DIR = (0.64, 0.48, 0.6)
AXES = ("zh", "y", "x", "zl", "c")
LANES, SUBS = 128, 8
PLANES = 8
TILES = 8
PITCH = 24
ROWS = PITCH * TILES + SUBS
MARGIN = 2
WIDE = PITCH * (TILES + 2 * MARGIN) + SUBS
TILE = (SUBS, LANES)
MIB = 1 << 20


def iota(axis):
    return lax.broadcasted_iota(jnp.int32, TILE, axis)


def take_lanes(values, index):
    return jnp.take_along_axis(values, index, axis=1)


def swap_groups(values, width):
    lane = iota(1)
    values = list(values)
    for bit in (1, 2, 4):
        low = (lane & (width * bit)) == 0
        for i in range(8):
            if not i & bit:
                a, b = values[i], values[i | bit]
                swapped = take_lanes(jnp.where(low, b, a), lane ^ (width * bit))
                values[i], values[i | bit] = jnp.where(low, a, swapped), jnp.where(low, swapped, b)
    return values


def dealt_columns(tiles):
    return swap_groups(tiles, 1)


def dealt_tile(tiles, at):
    lane = iota(1)
    if at < 0:
        moved = take_lanes(tiles[at + TILES], jnp.where(lane < 8, (lane + 119) & 127, lane - 8))
        return jnp.where(lane == 0, 0.0, moved)
    if at >= TILES:
        moved = take_lanes(tiles[at - TILES], jnp.where(lane < 120, lane + 8, (lane - 119) & 127))
        return jnp.where(lane == LANES - 1, 0.0, moved)
    return tiles[at]


def start_row(tile, half):
    return SUBS + PITCH * tile + SUBS * half


def smooth_plane(before, here, after, target, margin, scale=None):
    near, far = 0.25, 0.125
    if scale is not None:
        near, far = near * scale, far * scale

    def at(plane, row):
        return plane[0][plane[1], pl.ds(row, SUBS), :]

    for half in range(2):
        rows = [start_row(t, half) for t in range(TILES)]
        tiles = [at(here, r) for r in rows]
        done = []
        for t, r in enumerate(rows):
            beside = dealt_tile(tiles, t - 1) + dealt_tile(tiles, t + 1)
            beside += at(here, r - 1) + at(here, r + 1)
            beside += at(before, r) + at(after, r)
            done.append(near * tiles[t] + far * beside)
        for t in range(-margin, TILES + margin):
            target[0][target[1], pl.ds(start_row(t + margin, half), SUBS), :] = dealt_tile(done, t)


def clear_gaps(ref, margin):
    for t in range(TILES + 1):
        ref[:, pl.ds(PITCH * (t + margin), SUBS), :] = jnp.zeros((ref.shape[0], SUBS, LANES), jnp.float32)


def in_plane_gradients(at):
    rows_g = (at(1, 0) - at(-1, 0)) + 2.0 * (at(2, 0) - at(-2, 0))
    cols_g = (at(0, 1) - at(0, -1)) + 2.0 * (at(0, 2) - at(0, -2))
    facing = (0.9 * LIGHT_DIR[1]) * rows_g + (0.9 * LIGHT_DIR[2]) * cols_g
    return facing, rows_g * rows_g + cols_g * cols_g + 100.0


def fetch_kernel(density, materials, far, near, labels, sems):
    back = 4 * lax.axis_index("c")
    copies = [
        pltpu.make_async_copy(density.at[pl.ds(back, 4)], far, sems.at[0]),
        pltpu.make_async_copy(density.at[pl.ds(4 - back, 4)], near, sems.at[1]),
        pltpu.make_async_copy(materials, labels, sems.at[2]),
    ]
    for copy in copies:
        copy.start()
    for copy in copies:
        copy.wait()


def spread_plane(source, plane, target, place):
    for half in range(2):
        tiles = [source[plane, pl.ds(SUBS * half, SUBS), pl.ds(LANES * t, LANES)] for t in range(TILES)]
        for t, tile in enumerate(dealt_columns(tiles)):
            target[place, pl.ds(start_row(t, half), SUBS), :] = tile


def copy_plane(source, plane, target, place):
    for t in range(TILES):
        for half in range(2):
            rows = pl.ds(start_row(t, half), SUBS)
            target[place, rows, :] = source[plane, rows, :]


def inner_kernel(
    colors_hbm, opacity_hbm, far, near, labels, tint, scales, raw, once, twice, part, colors, opacity, sems
):
    copies = [
        pltpu.make_async_copy(colors_hbm, colors, sems.at[0]),
        pltpu.make_async_copy(opacity_hbm, opacity, sems.at[1]),
    ]
    for copy in copies:
        copy.start()
    clear_gaps(raw, 0)
    clear_gaps(once, 0)
    clear_gaps(twice, MARGIN)
    back = 4 * lax.axis_index("c")

    def spread(p, carry):
        spread_plane(far, p, raw, back + p)
        spread_plane(near, p, raw, 4 - back + p)
        return carry

    lax.fori_loop(0, 4, spread, 0)

    for copy in copies:
        copy.wait()
    lane, sub = iota(1), iota(0)
    tables = [jnp.zeros(TILE, jnp.float32) for _ in range(4)]
    for m in range(16):
        here = lane == m
        entries = (0.5 * opacity[m], colors[0, m], colors[1, m], colors[2, m])
        tables = [jnp.where(here, e, t) for e, t in zip(entries, tables)]

    def look(p, carry):
        for half in range(2):
            spans = []
            for span in range(2):
                cols = slice(LANES * span, LANES * (span + 1))
                a = jnp.broadcast_to(labels[p, 2 * half : 2 * half + 1, cols], TILE)
                b = jnp.broadcast_to(labels[p, 2 * half + 1 : 2 * half + 2, cols], TILE)
                spans.append(jnp.where(sub < 4, a, b))
            for side in range(2):
                from_lane = (lane & 3) * 32 + (lane >> 3) * 2 + side
                index = jnp.where((lane & 4) == 0, take_lanes(spans[0], from_lane), take_lanes(spans[1], from_lane))
                scales[side, 2 * p + half] = take_lanes(tables[0], index)
                for i in range(3):
                    tint[i, side, 2 * p + half] = take_lanes(tables[i + 1], index)
        return carry

    lax.fori_loop(0, PLANES, look, 0)

    def smooth_once(k, carry):
        smooth_plane((raw, k), (raw, k + 1), (raw, k + 2), (once, k), 0)
        return carry

    def smooth_twice(k, carry):
        smooth_plane((once, k), (once, k + 1), (once, k + 2), (twice, k), MARGIN)
        return carry

    lax.fori_loop(0, PLANES - 2, smooth_once, 0)
    lax.fori_loop(0, PLANES - 4, smooth_twice, 0)

    def grade(t, carry):
        start = pl.multiple_of(PITCH * t, SUBS) + PITCH * MARGIN
        for p in range(2, PLANES - 2):
            for half in range(2):

                def at(rows, tiles):
                    return twice[p - 2, pl.ds(start + start_row(tiles, half) + rows, SUBS), :]

                facing, length = in_plane_gradients(at)
                k = 2 * (p - 2) + half
                part[0, t, k] = facing
                part[1, t, k] = length
                scale = scales[t // 4, 2 * p + half]
                part[2, t, k] = scale + scale * jnp.tanh(at(0, 0))
        return carry

    lax.fori_loop(0, TILES, grade, 0)


def slab_kernel(far, near, tint, scales, raw, once, twice, part, out, raw_h, once_h, twice_h, layers):
    clear_gaps(raw_h, 0)
    clear_gaps(once_h, 0)
    clear_gaps(twice_h, MARGIN)
    core = lax.axis_index("c")
    position = lax.axis_index(AXES[0])
    total = lax.axis_size(AXES[0])
    for name in AXES[1:]:
        position = position * lax.axis_size(name) + lax.axis_index(name)
        total = total * lax.axis_size(name)
    sides = (core, 1 - core)
    outside = [jnp.where(position == side * (total - 1), 0.0, 1.0) for side in sides]
    for which, side in enumerate(sides):

        def plane(j, side=side):
            return side * (PLANES - 1) + (1 - 2 * side) * j

        for j in range(2):
            copy_plane(raw, plane(j), raw_h, 6 * which + 1 - j)
            copy_plane(once, plane(j + 1) - 1, once_h, 6 * which + 1 - j)

    def spread(k, carry):
        for which, (side, beyond) in enumerate(zip(sides, (far, near))):
            spread_plane(beyond, jnp.where(side == 0, 3 - k, k), raw_h, 6 * which + 2 + k)
        return carry

    def smooth_once(k, carry):
        for which in range(2):
            scale = jnp.where(k > 0, outside[which], 1.0)
            a = 6 * which + k
            smooth_plane((raw_h, a), (raw_h, a + 1), (raw_h, a + 2), (once_h, a + 2), 0, scale)
        return carry

    def smooth_twice(k, carry):
        for which in range(2):
            scale = jnp.where(k > 1, outside[which], 1.0)
            a = 6 * which + k
            smooth_plane((once_h, a), (once_h, a + 1), (once_h, a + 2), (twice_h, 4 * which + k), MARGIN, scale)
        return carry

    lax.fori_loop(0, 4, spread, 0)
    lax.fori_loop(0, 4, smooth_once, 0)
    lax.fori_loop(0, 4, smooth_twice, 0)

    def twice_at(p):
        if 2 <= p < PLANES - 2:
            return twice, p - 2
        return (twice_h, 4 * core + 1 - p) if p < 4 else (twice_h, 4 * (1 - core) + p - PLANES + 2)

    def shade(t, carry):
        start = pl.multiple_of(PITCH * t, SUBS) + PITCH * MARGIN
        side = t // 4
        found = [None, None]
        for p in range(PLANES):
            for half in range(2):

                def at(planes, rows, tiles):
                    ref, index = twice_at(p + planes)
                    return ref[index, pl.ds(start + start_row(tiles, half) + rows, SUBS), :]

                if 2 <= p < PLANES - 2:
                    facing, length, alpha = (part[i, t, 2 * (p - 2) + half] for i in range(3))
                else:
                    alpha = scales[side, 2 * p + half]
                    facing, length = in_plane_gradients(lambda rows, tiles: at(0, rows, tiles))
                    alpha = alpha + alpha * jnp.tanh(at(0, 0, 0))
                depth_g = (at(1, 0, 0) - at(-1, 0, 0)) + 2.0 * (at(2, 0, 0) - at(-2, 0, 0))
                facing = facing + (0.9 * LIGHT_DIR[0]) * depth_g
                length = length + depth_g * depth_g
                light = alpha * (0.1 + jnp.abs(facing) * lax.rsqrt(length))
                tints = [tint[i, side, 2 * p + half] for i in range(3)]
                if p == 0:
                    found[half] = [c * light for c in tints] + [1.0 - alpha]
                else:
                    transmit = found[half][3]
                    light = transmit * light
                    found[half] = [a + c * light for a, c in zip(found[half], tints)] + [
                        transmit - transmit * alpha
                    ]
        for half in range(2):
            for channel in range(4):
                layers[4 * half + channel, t] = found[half][channel]
        return carry

    lax.fori_loop(0, TILES, shade, 0)

    for half in range(2):
        for channel in range(4):
            tiles = [layers[4 * half + channel, t] for t in range(TILES)]
            for g, piece in enumerate(swap_groups(tiles, 16)):
                out[TILES * half + g, pl.ds(SUBS * channel, SUBS), :] = piece


def merge_kernel(parts, out):
    pieces = []
    for half in range(2):
        level = [
            [parts[8 * half + s, pl.ds(SUBS * channel, SUBS), :] for channel in range(4)] for s in range(8)
        ]
        while len(level) > 1:
            level = [
                [a[i] + a[3] * b[i] for i in range(3)] + [a[3] * b[3]] for a, b in zip(level[::2], level[1::2])
            ]
        pieces += level[0][:3] + [1.0 - level[0][3]]
    for g, piece in enumerate(swap_groups(pieces, 1)):
        out[pl.ds(g, SUBS, stride=SUBS), :] = piece


def final_kernel(parts, out):
    lane = iota(1)
    cover = lane | 3

    def over(front, back):
        return front + (1.0 - take_lanes(front, cover)) * back

    level = [parts[pl.ds(j, SUBS, stride=SUBS), :] for j in range(8)]
    while len(level) > 1:
        level = [over(a, b) for a, b in zip(level[::2], level[1::2])]
    value = level[0]
    for step in (1, 2, 4):
        value = over(value, pltpu.roll(value, SUBS - step, 0))
    value = over(value, pltpu.roll(value, LANES - 4, 1))
    value = 1.0 - jnp.exp(-4.0 * value)
    for channel in range(3):
        moved = take_lanes(value, 16 * (lane & 7) + (lane & 8) + channel)
        out[channel : channel + 1, :] = moved[0:1, 0:16]


VMEM_SPEC = pl.BlockSpec(memory_space=pltpu.VMEM)
HBM_SPEC = pl.BlockSpec(memory_space=pltpu.HBM)
INNER_OUT = (
    (3, 2, 2 * PLANES, SUBS, LANES),
    (2, 2 * PLANES, SUBS, LANES),
    (PLANES, ROWS, LANES),
    (PLANES - 2, ROWS, LANES),
    (PLANES - 4, WIDE, LANES),
    (3, TILES, 2 * (PLANES - 4), SUBS, LANES),
)
SLAB_SCRATCH = ((12, ROWS, LANES), (12, ROWS, LANES), (8, WIDE, LANES), (8, TILES, SUBS, LANES))


def run(kernel, shapes, scratch, in_specs, limit, cost=None):
    return pl.pallas_call(
        kernel,
        out_shape=[jax.ShapeDtypeStruct(s, d) for s, d in shapes],
        in_specs=in_specs,
        out_specs=[VMEM_SPEC] * len(shapes),
        scratch_shapes=scratch,
        compiler_params=pltpu.CompilerParams(vmem_limit_bytes=limit * MIB),
        cost_estimate=cost,
    )


def floats(*shapes):
    return [(s, jnp.float32) for s in shapes]


def vmem(*shapes):
    return [pltpu.VMEM(s, jnp.float32) for s in shapes]


def fetch(density, materials):
    edge = (4,) + density.shape[1:]
    shapes = floats(edge, edge) + [(materials.shape, materials.dtype)]
    return run(fetch_kernel, shapes, [pltpu.SemaphoreType.DMA((3,))], [HBM_SPEC] * 2, 4)(density, materials)


def render_inner(far, near, labels, colors, opacity):
    cost = pl.CostEstimate(flops=20_000_000, bytes_accessed=8_000_000, transcendentals=100_000)
    scratch = [
        pltpu.SMEM(colors.shape, jnp.float32),
        pltpu.SMEM(opacity.shape, jnp.float32),
        pltpu.SemaphoreType.DMA((2,)),
    ]
    specs = [HBM_SPEC] * 2 + [VMEM_SPEC] * 3
    return run(inner_kernel, floats(*INNER_OUT), scratch, specs, 16, cost)(
        colors, opacity, far, near, labels
    )


def render(far, near, inner):
    return run(slab_kernel, floats((16, 32, LANES)), vmem(*SLAB_SCRATCH), [VMEM_SPEC] * 8, 16)(far, near, *inner)[0]


def on_device(density, materials, colors, opacity):
    size = lax.axis_size(AXES)
    beside = [(i, i ^ 1) for i in range(size)]
    across = [(i, i + 1) for i in range(1, size - 1, 2)]
    across += [(b, a) for a, b in across]
    density, materials, colors, opacity = (
        pltpu.with_memory_space_constraint(a, pltpu.HBM) for a in (density, materials, colors, opacity)
    )
    far, near, labels = fetch(density, materials)
    inner = render_inner(far, near, labels, colors, opacity)
    far = lax.ppermute(far, AXES, across)
    near = lax.ppermute(near, AXES, beside)
    pieces = render(far, near, inner)
    parts = lax.all_to_all(pieces, ("zh", "zl", "c"), split_axis=0, concat_axis=0, tiled=True)
    rows = run(merge_kernel, floats((64, LANES)), (), [VMEM_SPEC], 2)(parts)[0]
    rows = lax.all_to_all(rows, ("y", "x"), split_axis=0, concat_axis=0, tiled=True)
    return run(final_kernel, floats((3, 16)), (), [VMEM_SPEC], 2)(rows)[0]


def solution(mesh):
    grid = Mesh(mesh.devices.reshape(2, 8, 8, 4, 2), AXES)
    placed = (P(AXES, None, None), P(AXES, None, None), P(), P())
    return jax.shard_map(on_device, mesh=grid, in_specs=placed, out_specs=P(None, AXES), check_vma=False)
```

```python
import jax
import jax.numpy as jnp
from jax import lax
from jax.experimental import pallas as pl
from jax.experimental.pallas import tpu as pltpu
from jax.sharding import Mesh, PartitionSpec as P


LIGHT_DIR = (0.64, 0.48, 0.6)
AXES = ("zh", "y", "x", "zl", "c")
LANES, SUBS = 128, 8
PLANES = 8
TILES = 8
PITCH = 24
ROWS = PITCH * TILES + SUBS
WIDE = PITCH * (TILES + 2) + SUBS
TILE = (SUBS, LANES)
MIB = 1 << 20


def iota(axis):
    return lax.broadcasted_iota(jnp.int32, TILE, axis)


def take_lanes(values, index):
    return jnp.take_along_axis(values, index, axis=1)


def shift_columns(tiles, at, by):
    lane = iota(1)
    if by < 0:
        beside = tiles[at - 1] if at else jnp.zeros(TILE, jnp.float32)
        mixed = jnp.where(lane >= LANES + by, beside, tiles[at])
    else:
        beside = tiles[at + 1] if at + 1 < len(tiles) else jnp.zeros(TILE, jnp.float32)
        mixed = jnp.where(lane < by, beside, tiles[at])
    return pltpu.roll(mixed, (-by) % LANES, 1)


def start_row(tile, half):
    return SUBS + PITCH * tile + SUBS * half


def smooth_plane(before, here, after, target, pad, scale=None):
    near, far = 0.25, 0.125
    if scale is not None:
        near, far = near * scale, far * scale

    def at(plane, row):
        return plane[0][plane[1], pl.ds(row, SUBS), :]

    for half in range(2):
        rows = [start_row(t, half) for t in range(TILES)]
        tiles = [at(here, r) for r in rows]
        for t, r in enumerate(rows):
            beside = shift_columns(tiles, t, -1) + shift_columns(tiles, t, 1)
            beside += at(here, r - 1) + at(here, r + 1)
            beside += at(before, r) + at(after, r)
            target[0][target[1], pl.ds(r + pad, SUBS), :] = near * tiles[t] + far * beside


def clear_gaps(ref, wide):
    shape = (ref.shape[0], SUBS, LANES)
    for t in range(TILES + 1 + 2 * wide):
        ref[:, pl.ds(PITCH * t, SUBS), :] = jnp.zeros(shape, jnp.float32)
    if wide:
        for t in (0, TILES + 1):
            for half in range(2):
                ref[:, pl.ds(start_row(t, half), SUBS), :] = jnp.zeros(shape, jnp.float32)


def transposed_groups(values):
    group = iota(1) // 16
    values = list(values)
    for bit in (1, 2, 4):
        low = (group & bit) == 0
        for i in range(8):
            if not i & bit:
                a, b = values[i], values[i | bit]
                values[i] = jnp.where(low, a, pltpu.roll(b, 16 * bit, 1))
                values[i | bit] = jnp.where(low, pltpu.roll(a, LANES - 16 * bit, 1), b)
    return values


def in_plane_gradients(at):
    row = [at(0, -1), at(0, 0), at(0, 1)]
    rows_g = (at(1, 0) - at(-1, 0)) + 2.0 * (at(2, 0) - at(-2, 0))
    cols_g = (shift_columns(row, 1, 1) - shift_columns(row, 1, -1)) + 2.0 * (
        shift_columns(row, 1, 2) - shift_columns(row, 1, -2)
    )
    facing = (0.9 * LIGHT_DIR[1]) * rows_g + (0.9 * LIGHT_DIR[2]) * cols_g
    return facing, rows_g * rows_g + cols_g * cols_g + 100.0


def lead_kernel(density, far, sem):
    copy = pltpu.make_async_copy(density.at[pl.ds(4 * lax.axis_index("c"), 4)], far, sem)
    copy.start()
    copy.wait()


def rest_kernel(density, materials, near, labels, sems):
    copies = [
        pltpu.make_async_copy(density.at[pl.ds(4 - 4 * lax.axis_index("c"), 4)], near, sems.at[0]),
        pltpu.make_async_copy(materials, labels, sems.at[1]),
    ]
    for copy in copies:
        copy.start()
    for copy in copies:
        copy.wait()


def spread_planes(source, target, place):
    for p in range(4):
        for t in range(TILES):
            for half in range(2):
                target[place(p), pl.ds(start_row(t, half), SUBS), :] = source[
                    p, pl.ds(SUBS * half, SUBS), pl.ds(LANES * t, LANES)
                ]


def inner_kernel(
    colors_hbm, opacity_hbm, far, near, labels, tint, alphas, raw, once, twice, part, looked, colors, opacity, sems
):
    copies = [
        pltpu.make_async_copy(colors_hbm, colors, sems.at[0]),
        pltpu.make_async_copy(opacity_hbm, opacity, sems.at[1]),
    ]
    for copy in copies:
        copy.start()
    clear_gaps(raw, 0)
    clear_gaps(once, 0)
    clear_gaps(twice, 1)
    back = 4 * lax.axis_index("c")
    spread_planes(far, raw, lambda p: back + p)
    spread_planes(near, raw, lambda p: 4 - back + p)

    for copy in copies:
        copy.wait()
    lane, sub = iota(1), iota(0)
    tables = [jnp.zeros(TILE, jnp.float32) for _ in range(4)]
    for m in range(16):
        here = lane == m
        entries = (0.5 * opacity[m], colors[0, m], colors[1, m], colors[2, m])
        tables = [jnp.where(here, e, t) for e, t in zip(entries, tables)]

    def look(p, carry):
        for half in range(2):
            for side in range(2):
                cols = slice(LANES * side, LANES * (side + 1))
                a = jnp.broadcast_to(labels[p, 2 * half : 2 * half + 1, cols], TILE)
                b = jnp.broadcast_to(labels[p, 2 * half + 1 : 2 * half + 2, cols], TILE)
                index = jnp.where(sub < 4, a, b)
                for i, table in enumerate(tables):
                    looked[i, side, 2 * p + half] = take_lanes(table, index)
        return carry

    each(PLANES, 4, lambda p: look(p, 0))

    def smooth_once(p, carry):
        smooth_plane((raw, p - 1), (raw, p), (raw, p + 1), (once, p - 1), 0)
        return carry

    def smooth_twice(p, carry):
        smooth_plane((once, p - 2), (once, p - 1), (once, p), (twice, p - 2), PITCH)
        return carry

    for p in range(1, PLANES - 1):
        smooth_once(p, 0)
    for p in range(2, PLANES - 2):
        smooth_twice(p, 0)

    def spread_tile(t, carry):
        side = t // 4
        spread = (t % 4) * 32 + lane // 4
        start = pl.multiple_of(PITCH * t, SUBS) + PITCH
        for p in range(PLANES):
            for half in range(2):
                scale, *tints = [take_lanes(looked[i, side, 2 * p + half], spread) for i in range(4)]
                for i, value in enumerate(tints):
                    tint[i, t, 2 * p + half] = value
                if 2 <= p < PLANES - 2:

                    def at(rows, tiles):
                        return twice[p - 2, pl.ds(start + start_row(tiles, half) + rows, SUBS), :]

                    facing, length = in_plane_gradients(at)
                    part[0, t, 2 * p + half] = facing
                    part[1, t, 2 * p + half] = length
                    scale = scale + scale * jnp.tanh(at(0, 0))
                alphas[t, 2 * p + half] = scale
        return carry

    each(TILES, 4, lambda t: spread_tile(t, 0))


def render_half(side, beyond, tint, alphas, raw, once, twice, part, raw_h, once_h, twice_h, shades):
    clear_gaps(raw_h, 0)
    clear_gaps(once_h, 0)
    clear_gaps(twice_h, 1)
    spread_planes(beyond, raw_h, lambda p: jnp.where(side == 0, 3 - p, p))
    position = lax.axis_index(AXES[0])
    total = lax.axis_size(AXES[0])
    for name in AXES[1:]:
        position = position * lax.axis_size(name) + lax.axis_index(name)
        total = total * lax.axis_size(name)
    outside = jnp.where(position == side * (total - 1), 0.0, 1.0)
    step = 1 - 2 * side

    def plane(j):
        return side * (PLANES - 1) + step * j

    def raw_at(j):
        return (raw, plane(j)) if j >= 0 else (raw_h, -1 - j)

    def once_at(j):
        return (once, plane(j) - 1) if j >= 1 else (once_h, -j)

    def twice_at(j):
        return (twice, plane(j) - 2) if j >= 2 else (twice_h, 1 - j)

    for j in (-3, -2, -1, 0):
        smooth_plane(raw_at(j - 1), raw_at(j), raw_at(j + 1), once_at(j), 0, outside if j < 0 else None)
    for j in (-2, -1, 0, 1):
        smooth_plane(once_at(j - 1), once_at(j), once_at(j + 1), twice_at(j), PITCH, outside if j < 0 else None)
    depth_weight = (0.9 * LIGHT_DIR[0]) * step.astype(jnp.float32)

    def shade(t):
        start = pl.multiple_of(PITCH * t, SUBS) + PITCH
        for j in range(4):
            p = plane(j)
            for half in range(2):

                def at(planes, rows, tiles):
                    ref, index = twice_at(j + planes)
                    return ref[index, pl.ds(start + start_row(tiles, half) + rows, SUBS), :]

                alpha = alphas[t, 2 * p + half]
                if j >= 2:
                    facing, length = (part[i, t, 2 * p + half] for i in range(2))
                else:
                    facing, length = in_plane_gradients(lambda rows, tiles: at(0, rows, tiles))
                    alpha = alpha + alpha * jnp.tanh(at(0, 0, 0))
                depth_g = (at(1, 0, 0) - at(-1, 0, 0)) + 2.0 * (at(2, 0, 0) - at(-2, 0, 0))
                facing = facing + depth_weight * depth_g
                length = length + depth_g * depth_g
                k = p - 4 * side
                shades[2 * half, k] = alpha
                shades[2 * half + 1, k] = alpha * (0.1 + jnp.abs(facing) * lax.rsqrt(length))
        found = []
        for half in range(2):
            for k in range(4):
                alpha, light = shades[2 * half, k], shades[2 * half + 1, k]
                tints = [tint[i, t, 2 * (k + 4 * side) + half] for i in range(3)]
                if k == 0:
                    layer = [c * light for c in tints] + [1.0 - alpha]
                else:
                    transmit = layer[3]
                    light = transmit * light
                    layer = [a + c * light for a, c in zip(layer, tints)] + [transmit - transmit * alpha]
            found.append(layer)
        return found

    return shade


def near_kernel(beyond, tint, alphas, raw, once, twice, part, layers, *scratch):
    shade = render_half(1 - lax.axis_index("c"), beyond, tint, alphas, raw, once, twice, part, *scratch)

    def body(t, carry):
        for half, layer in enumerate(shade(t)):
            for channel, value in enumerate(layer):
                layers[4 * half + channel, t] = value
        return carry

    each(TILES, 4, lambda t: body(t, 0))


def far_kernel(beyond, tint, alphas, raw, once, twice, part, others, out, layers, *scratch):
    side = lax.axis_index("c")
    shade = render_half(side, beyond, tint, alphas, raw, once, twice, part, *scratch)

    def body(t, carry):
        for half, layer in enumerate(shade(t)):
            other = [others[4 * half + channel, t] for channel in range(4)]
            front = [jnp.where(side == 0, a, b) for a, b in zip(layer, other)]
            back = [jnp.where(side == 0, b, a) for a, b in zip(layer, other)]
            for channel in range(4):
                value = front[3] * back[channel]
                layers[4 * half + channel, t] = value if channel == 3 else front[channel] + value
        return carry

    each(TILES, 4, lambda t: body(t, 0))
    for half in range(2):
        for channel in range(4):
            tiles = [layers[4 * half + channel, t] for t in range(TILES)]
            for g, piece in enumerate(transposed_groups(tiles)):
                out[TILES * half + g, pl.ds(SUBS * channel, SUBS), :] = piece


def merge_kernel(parts, out):
    pieces = []
    for half in range(2):
        level = [
            [parts[8 * half + s, pl.ds(SUBS * channel, SUBS), :] for channel in range(4)] for s in range(8)
        ]
        while len(level) > 1:
            level = [
                [a[i] + a[3] * b[i] for i in range(3)] + [a[3] * b[3]] for a, b in zip(level[::2], level[1::2])
            ]
        pieces += level[0][:3] + [1.0 - level[0][3]]
    for g, piece in enumerate(transposed_groups(pieces)):
        out[pl.ds(g, SUBS, stride=SUBS), :] = piece


def final_kernel(parts, out):
    lane = iota(1)
    cover = (lane & 64) + 48 + lane % 16

    def over(front, back):
        return front + (1.0 - take_lanes(front, cover)) * back

    level = [parts[pl.ds(j, SUBS, stride=SUBS), :] for j in range(8)]
    while len(level) > 1:
        level = [over(a, b) for a, b in zip(level[::2], level[1::2])]
    value = level[0]
    for step in (1, 2, 4):
        value = over(value, pltpu.roll(value, SUBS - step, 0))
    value = over(value, pltpu.roll(value, 64, 1))
    value = 1.0 - jnp.exp(-4.0 * value)
    for channel in range(3):
        moved = pltpu.roll(value, LANES - 16 * channel, 1) if channel else value
        out[channel : channel + 1, :] = moved[0:1, 0:16]


VMEM_SPEC = pl.BlockSpec(memory_space=pltpu.VMEM)
HBM_SPEC = pl.BlockSpec(memory_space=pltpu.HBM)
RAW, ONCE, TWICE = (PLANES, ROWS, LANES), (PLANES - 2, ROWS, LANES), (PLANES - 4, WIDE, LANES)
SHADED = (TILES, 2 * PLANES, SUBS, LANES)
LAYERS = (8, TILES, SUBS, LANES)
HALF = ((4, ROWS, LANES), (4, ROWS, LANES), (4, WIDE, LANES), (4, 4, SUBS, LANES))


def each(count, together, body):
    def turn(k, carry):
        for m in range(together):
            body(together * k + m)
        return carry

    lax.fori_loop(0, count // together, turn, 0)


def run(kernel, shapes, scratch, in_specs, limit, cost=None):
    return pl.pallas_call(
        kernel,
        out_shape=[jax.ShapeDtypeStruct(s, d) for s, d in shapes],
        in_specs=in_specs,
        out_specs=[VMEM_SPEC] * len(shapes),
        scratch_shapes=scratch,
        compiler_params=pltpu.CompilerParams(vmem_limit_bytes=limit * MIB),
        cost_estimate=cost,
    )


def floats(*shapes):
    return [(s, jnp.float32) for s in shapes]


def vmem(*shapes):
    return [pltpu.VMEM(s, jnp.float32) for s in shapes]


def fetch(density, materials):
    edge = (4,) + density.shape[1:]
    cost = pl.CostEstimate(flops=0, bytes_accessed=600_000, transcendentals=0)
    far = run(lead_kernel, floats(edge), [pltpu.SemaphoreType.DMA], [HBM_SPEC], 4)(density)[0]
    shapes = floats(edge) + [(materials.shape, materials.dtype)]
    near, labels = run(rest_kernel, shapes, [pltpu.SemaphoreType.DMA((2,))], [HBM_SPEC] * 2, 4, cost)(
        density, materials
    )
    return far, near, labels


def render_inner(far, near, labels, colors, opacity):
    cost = pl.CostEstimate(flops=20_000_000, bytes_accessed=8_000_000, transcendentals=100_000)
    scratch = vmem((4, 2, 2 * PLANES, SUBS, LANES)) + [
        pltpu.SMEM(colors.shape, jnp.float32),
        pltpu.SMEM(opacity.shape, jnp.float32),
        pltpu.SemaphoreType.DMA((2,)),
    ]
    specs = [HBM_SPEC] * 2 + [VMEM_SPEC] * 3
    shapes = floats((3,) + SHADED, SHADED, RAW, ONCE, TWICE, (2,) + SHADED)
    return run(inner_kernel, shapes, scratch, specs, 16, cost)(colors, opacity, far, near, labels)


def render(far, near, inner):
    cost = pl.CostEstimate(flops=5_000_000, bytes_accessed=4_000_000, transcendentals=50_000)
    layers = run(near_kernel, floats(LAYERS), vmem(*HALF), [VMEM_SPEC] * 7, 16, cost)(near, *inner)
    pieces = floats((16, 32, LANES))
    return run(far_kernel, pieces, vmem(LAYERS, *HALF), [VMEM_SPEC] * 8, 16)(far, *inner, layers[0])[0]


def on_device(density, materials, colors, opacity):
    size = lax.axis_size(AXES)
    beside = [(i, i ^ 1) for i in range(size)]
    across = [(i, i + 1) for i in range(1, size - 1, 2)]
    across += [(b, a) for a, b in across]
    density, materials, colors, opacity = (
        pltpu.with_memory_space_constraint(a, pltpu.HBM) for a in (density, materials, colors, opacity)
    )
    far, near, labels = fetch(density, materials)
    inner = render_inner(far, near, labels, colors, opacity)
    far = lax.ppermute(far, AXES, across)
    near = lax.ppermute(near, AXES, beside)
    pieces = render(far, near, inner)
    parts = lax.all_to_all(pieces, ("zh", "zl", "c"), split_axis=0, concat_axis=0, tiled=True)
    rows = run(merge_kernel, floats((64, LANES)), (), [VMEM_SPEC], 2)(parts)[0]
    rows = lax.all_to_all(rows, ("y", "x"), split_axis=0, concat_axis=0, tiled=True)
    return run(final_kernel, floats((3, 16)), (), [VMEM_SPEC], 2)(rows)[0]


def solution(mesh):
    grid = Mesh(mesh.devices.reshape(2, 8, 8, 4, 2), AXES)
    placed = (P(AXES, None, None), P(AXES, None, None), P(), P())
    return jax.shard_map(on_device, mesh=grid, in_specs=placed, out_specs=P(None, AXES), check_vma=False)
```

```python
import jax
import jax.numpy as jnp
from jax import lax
from jax.experimental import pallas as pl
from jax.experimental.pallas import tpu as pltpu
from jax.sharding import Mesh, PartitionSpec as P


LIGHT_DIR = (0.64, 0.48, 0.6)
AXES = ("zh", "y", "x", "zl", "c")
LANES, SUBS = 128, 8
PLANES = 8
TILES = 8
PITCH = 24
ROWS = PITCH * TILES + SUBS
WIDE = PITCH * (TILES + 2) + SUBS
TILE = (SUBS, LANES)
MIB = 1 << 20


def iota(axis):
    return lax.broadcasted_iota(jnp.int32, TILE, axis)


def take_lanes(values, index):
    return jnp.take_along_axis(values, index, axis=1)


def shift_columns(tiles, at, by):
    lane = iota(1)
    if by < 0:
        beside = tiles[at - 1] if at else jnp.zeros(TILE, jnp.float32)
        mixed = jnp.where(lane >= LANES + by, beside, tiles[at])
    else:
        beside = tiles[at + 1] if at + 1 < len(tiles) else jnp.zeros(TILE, jnp.float32)
        mixed = jnp.where(lane < by, beside, tiles[at])
    return pltpu.roll(mixed, (-by) % LANES, 1)


def start_row(tile, half):
    return SUBS + PITCH * tile + SUBS * half


def smooth_plane(before, here, after, target, pad, scale=None):
    near, far = 0.25, 0.125
    if scale is not None:
        near, far = near * scale, far * scale

    def at(plane, row):
        return plane[0][plane[1], pl.ds(row, SUBS), :]

    for half in range(2):
        rows = [start_row(t, half) for t in range(TILES)]
        tiles = [at(here, r) for r in rows]
        for t, r in enumerate(rows):
            beside = shift_columns(tiles, t, -1) + shift_columns(tiles, t, 1)
            beside += at(here, r - 1) + at(here, r + 1)
            beside += at(before, r) + at(after, r)
            target[0][target[1], pl.ds(r + pad, SUBS), :] = near * tiles[t] + far * beside


def clear_gaps(ref, wide):
    shape = (ref.shape[0], SUBS, LANES)
    for t in range(TILES + 1 + 2 * wide):
        ref[:, pl.ds(PITCH * t, SUBS), :] = jnp.zeros(shape, jnp.float32)
    if wide:
        for t in (0, TILES + 1):
            for half in range(2):
                ref[:, pl.ds(start_row(t, half), SUBS), :] = jnp.zeros(shape, jnp.float32)


def transposed_groups(values):
    group = iota(1) // 16
    values = list(values)
    for bit in (1, 2, 4):
        low = (group & bit) == 0
        for i in range(8):
            if not i & bit:
                a, b = values[i], values[i | bit]
                values[i] = jnp.where(low, a, pltpu.roll(b, 16 * bit, 1))
                values[i | bit] = jnp.where(low, pltpu.roll(a, LANES - 16 * bit, 1), b)
    return values


def in_plane_gradients(at):
    row = [at(0, -1), at(0, 0), at(0, 1)]
    rows_g = (at(1, 0) - at(-1, 0)) + 2.0 * (at(2, 0) - at(-2, 0))
    cols_g = (shift_columns(row, 1, 1) - shift_columns(row, 1, -1)) + 2.0 * (
        shift_columns(row, 1, 2) - shift_columns(row, 1, -2)
    )
    facing = (0.9 * LIGHT_DIR[1]) * rows_g + (0.9 * LIGHT_DIR[2]) * cols_g
    return facing, rows_g * rows_g + cols_g * cols_g + 100.0


def fetch_kernel(density, materials, far, near, labels, sems):
    back = 4 * lax.axis_index("c")
    copies = [
        pltpu.make_async_copy(density.at[pl.ds(back, 4)], far, sems.at[0]),
        pltpu.make_async_copy(density.at[pl.ds(4 - back, 4)], near, sems.at[1]),
        pltpu.make_async_copy(materials, labels, sems.at[2]),
    ]
    for copy in copies:
        copy.start()
    for copy in copies:
        copy.wait()


def spread_planes(source, target, place):
    for p in range(4):
        for t in range(TILES):
            for half in range(2):
                target[place(p), pl.ds(start_row(t, half), SUBS), :] = source[
                    p, pl.ds(SUBS * half, SUBS), pl.ds(LANES * t, LANES)
                ]


def inner_kernel(
    colors_hbm, opacity_hbm, far, near, labels, tint, alphas, raw, once, twice, part, looked, colors, opacity, sems
):
    copies = [
        pltpu.make_async_copy(colors_hbm, colors, sems.at[0]),
        pltpu.make_async_copy(opacity_hbm, opacity, sems.at[1]),
    ]
    for copy in copies:
        copy.start()
    clear_gaps(raw, 0)
    clear_gaps(once, 0)
    clear_gaps(twice, 1)
    back = 4 * lax.axis_index("c")
    spread_planes(far, raw, lambda p: back + p)
    spread_planes(near, raw, lambda p: 4 - back + p)

    for copy in copies:
        copy.wait()
    lane, sub = iota(1), iota(0)
    tables = [jnp.zeros(TILE, jnp.float32) for _ in range(4)]
    for m in range(16):
        here = lane == m
        entries = (0.5 * opacity[m], colors[0, m], colors[1, m], colors[2, m])
        tables = [jnp.where(here, e, t) for e, t in zip(entries, tables)]

    def look(p, carry):
        for half in range(2):
            for side in range(2):
                cols = slice(LANES * side, LANES * (side + 1))
                a = jnp.broadcast_to(labels[p, 2 * half : 2 * half + 1, cols], TILE)
                b = jnp.broadcast_to(labels[p, 2 * half + 1 : 2 * half + 2, cols], TILE)
                index = jnp.where(sub < 4, a, b)
                for i, table in enumerate(tables):
                    looked[i, side, 2 * p + half] = take_lanes(table, index)
        return carry

    each(PLANES, 8, lambda p: look(p, 0))

    def smooth_once(p, carry):
        smooth_plane((raw, p - 1), (raw, p), (raw, p + 1), (once, p - 1), 0)
        return carry

    def smooth_twice(p, carry):
        smooth_plane((once, p - 2), (once, p - 1), (once, p), (twice, p - 2), PITCH)
        return carry

    for p in range(1, PLANES - 1):
        smooth_once(p, 0)
    for p in range(2, PLANES - 2):
        smooth_twice(p, 0)

    def spread_tile(t, carry):
        side = t // 4
        spread = (t % 4) * 32 + lane // 4
        start = pl.multiple_of(PITCH * t, SUBS) + PITCH
        for p in range(PLANES):
            for half in range(2):
                scale, *tints = [take_lanes(looked[i, side, 2 * p + half], spread) for i in range(4)]
                for i, value in enumerate(tints):
                    tint[i, t, 2 * p + half] = value
                if 2 <= p < PLANES - 2:

                    def at(rows, tiles):
                        return twice[p - 2, pl.ds(start + start_row(tiles, half) + rows, SUBS), :]

                    facing, length = in_plane_gradients(at)
                    part[0, t, 2 * p + half] = facing
                    part[1, t, 2 * p + half] = length
                    scale = scale + scale * jnp.tanh(at(0, 0))
                alphas[t, 2 * p + half] = scale
        return carry

    each(TILES, 4, lambda t: spread_tile(t, 0))


def render_half(side, beyond, tint, alphas, raw, once, twice, part, raw_h, once_h, twice_h, shades):
    clear_gaps(raw_h, 0)
    clear_gaps(once_h, 0)
    clear_gaps(twice_h, 1)
    spread_planes(beyond, raw_h, lambda p: jnp.where(side == 0, 3 - p, p))
    position = lax.axis_index(AXES[0])
    total = lax.axis_size(AXES[0])
    for name in AXES[1:]:
        position = position * lax.axis_size(name) + lax.axis_index(name)
        total = total * lax.axis_size(name)
    outside = jnp.where(position == side * (total - 1), 0.0, 1.0)
    step = 1 - 2 * side

    def plane(j):
        return side * (PLANES - 1) + step * j

    def raw_at(j):
        return (raw, plane(j)) if j >= 0 else (raw_h, -1 - j)

    def once_at(j):
        return (once, plane(j) - 1) if j >= 1 else (once_h, -j)

    def twice_at(j):
        return (twice, plane(j) - 2) if j >= 2 else (twice_h, 1 - j)

    for j in (-3, -2, -1, 0):
        smooth_plane(raw_at(j - 1), raw_at(j), raw_at(j + 1), once_at(j), 0, outside if j < 0 else None)
    for j in (-2, -1, 0, 1):
        smooth_plane(once_at(j - 1), once_at(j), once_at(j + 1), twice_at(j), PITCH, outside if j < 0 else None)
    depth_weight = (0.9 * LIGHT_DIR[0]) * step.astype(jnp.float32)

    def shade(t):
        start = pl.multiple_of(PITCH * t, SUBS) + PITCH
        for j in range(4):
            p = plane(j)
            for half in range(2):

                def at(planes, rows, tiles):
                    ref, index = twice_at(j + planes)
                    return ref[index, pl.ds(start + start_row(tiles, half) + rows, SUBS), :]

                alpha = alphas[t, 2 * p + half]
                if j >= 2:
                    facing, length = (part[i, t, 2 * p + half] for i in range(2))
                else:
                    facing, length = in_plane_gradients(lambda rows, tiles: at(0, rows, tiles))
                    alpha = alpha + alpha * jnp.tanh(at(0, 0, 0))
                depth_g = (at(1, 0, 0) - at(-1, 0, 0)) + 2.0 * (at(2, 0, 0) - at(-2, 0, 0))
                facing = facing + depth_weight * depth_g
                length = length + depth_g * depth_g
                k = p - 4 * side
                shades[2 * half, k] = alpha
                shades[2 * half + 1, k] = alpha * (0.1 + jnp.abs(facing) * lax.rsqrt(length))
        found = []
        for half in range(2):
            for k in range(4):
                alpha, light = shades[2 * half, k], shades[2 * half + 1, k]
                tints = [tint[i, t, 2 * (k + 4 * side) + half] for i in range(3)]
                if k == 0:
                    layer = [c * light for c in tints] + [1.0 - alpha]
                else:
                    transmit = layer[3]
                    light = transmit * light
                    layer = [a + c * light for a, c in zip(layer, tints)] + [transmit - transmit * alpha]
            found.append(layer)
        return found

    return shade


def near_kernel(beyond, tint, alphas, raw, once, twice, part, layers, *scratch):
    shade = render_half(1 - lax.axis_index("c"), beyond, tint, alphas, raw, once, twice, part, *scratch)

    def body(t, carry):
        for half, layer in enumerate(shade(t)):
            for channel, value in enumerate(layer):
                layers[4 * half + channel, t] = value
        return carry

    each(TILES, 8, lambda t: body(t, 0))


def far_kernel(beyond, tint, alphas, raw, once, twice, part, others, out, layers, *scratch):
    side = lax.axis_index("c")
    shade = render_half(side, beyond, tint, alphas, raw, once, twice, part, *scratch)

    def body(t, carry):
        for half, layer in enumerate(shade(t)):
            other = [others[4 * half + channel, t] for channel in range(4)]
            front = [jnp.where(side == 0, a, b) for a, b in zip(layer, other)]
            back = [jnp.where(side == 0, b, a) for a, b in zip(layer, other)]
            for channel in range(4):
                value = front[3] * back[channel]
                layers[4 * half + channel, t] = value if channel == 3 else front[channel] + value
        return carry

    each(TILES, 4, lambda t: body(t, 0))
    for half in range(2):
        for channel in range(4):
            tiles = [layers[4 * half + channel, t] for t in range(TILES)]
            for g, piece in enumerate(transposed_groups(tiles)):
                out[TILES * half + g, pl.ds(SUBS * channel, SUBS), :] = piece


def merge_kernel(parts, out):
    pieces = []
    for half in range(2):
        level = [
            [parts[8 * half + s, pl.ds(SUBS * channel, SUBS), :] for channel in range(4)] for s in range(8)
        ]
        while len(level) > 1:
            level = [
                [a[i] + a[3] * b[i] for i in range(3)] + [a[3] * b[3]] for a, b in zip(level[::2], level[1::2])
            ]
        pieces += level[0][:3] + [1.0 - level[0][3]]
    for g, piece in enumerate(transposed_groups(pieces)):
        out[pl.ds(g, SUBS, stride=SUBS), :] = piece


def final_kernel(parts, out):
    lane = iota(1)
    cover = (lane & 64) + 48 + lane % 16

    def over(front, back):
        return front + (1.0 - take_lanes(front, cover)) * back

    level = [parts[pl.ds(j, SUBS, stride=SUBS), :] for j in range(8)]
    while len(level) > 1:
        level = [over(a, b) for a, b in zip(level[::2], level[1::2])]
    value = level[0]
    for step in (1, 2, 4):
        value = over(value, pltpu.roll(value, SUBS - step, 0))
    value = over(value, pltpu.roll(value, 64, 1))
    value = 1.0 - jnp.exp(-4.0 * value)
    for channel in range(3):
        moved = pltpu.roll(value, LANES - 16 * channel, 1) if channel else value
        out[channel : channel + 1, :] = moved[0:1, 0:16]


VMEM_SPEC = pl.BlockSpec(memory_space=pltpu.VMEM)
HBM_SPEC = pl.BlockSpec(memory_space=pltpu.HBM)
RAW, ONCE, TWICE = (PLANES, ROWS, LANES), (PLANES - 2, ROWS, LANES), (PLANES - 4, WIDE, LANES)
SHADED = (TILES, 2 * PLANES, SUBS, LANES)
LAYERS = (8, TILES, SUBS, LANES)
HALF = ((4, ROWS, LANES), (4, ROWS, LANES), (4, WIDE, LANES), (4, 4, SUBS, LANES))


def each(count, together, body):
    def turn(k, carry):
        for m in range(together):
            body(together * k + m)
        return carry

    lax.fori_loop(0, count // together, turn, 0)


def run(kernel, shapes, scratch, in_specs, limit, cost=None):
    return pl.pallas_call(
        kernel,
        out_shape=[jax.ShapeDtypeStruct(s, d) for s, d in shapes],
        in_specs=in_specs,
        out_specs=[VMEM_SPEC] * len(shapes),
        scratch_shapes=scratch,
        compiler_params=pltpu.CompilerParams(vmem_limit_bytes=limit * MIB),
        cost_estimate=cost,
    )


def floats(*shapes):
    return [(s, jnp.float32) for s in shapes]


def vmem(*shapes):
    return [pltpu.VMEM(s, jnp.float32) for s in shapes]


def fetch(density, materials):
    edge = (4,) + density.shape[1:]
    shapes = floats(edge, edge) + [(materials.shape, materials.dtype)]
    return run(fetch_kernel, shapes, [pltpu.SemaphoreType.DMA((3,))], [HBM_SPEC] * 2, 4)(density, materials)


def render_inner(far, near, labels, colors, opacity):
    cost = pl.CostEstimate(flops=20_000_000, bytes_accessed=8_000_000, transcendentals=100_000)
    scratch = vmem((4, 2, 2 * PLANES, SUBS, LANES)) + [
        pltpu.SMEM(colors.shape, jnp.float32),
        pltpu.SMEM(opacity.shape, jnp.float32),
        pltpu.SemaphoreType.DMA((2,)),
    ]
    specs = [HBM_SPEC] * 2 + [VMEM_SPEC] * 3
    shapes = floats((3,) + SHADED, SHADED, RAW, ONCE, TWICE, (2,) + SHADED)
    return run(inner_kernel, shapes, scratch, specs, 16, cost)(colors, opacity, far, near, labels)


def render(far, near, inner):
    cost = pl.CostEstimate(flops=5_000_000, bytes_accessed=4_000_000, transcendentals=50_000)
    layers = run(near_kernel, floats(LAYERS), vmem(*HALF), [VMEM_SPEC] * 7, 16, cost)(near, *inner)
    pieces = floats((16, 32, LANES))
    return run(far_kernel, pieces, vmem(LAYERS, *HALF), [VMEM_SPEC] * 8, 16)(far, *inner, layers[0])[0]


def on_device(density, materials, colors, opacity):
    size = lax.axis_size(AXES)
    beside = [(i, i ^ 1) for i in range(size)]
    across = [(i, i + 1) for i in range(1, size - 1, 2)]
    across += [(b, a) for a, b in across]
    density, materials, colors, opacity = (
        pltpu.with_memory_space_constraint(a, pltpu.HBM) for a in (density, materials, colors, opacity)
    )
    far, near, labels = fetch(density, materials)
    inner = render_inner(far, near, labels, colors, opacity)
    far = lax.ppermute(far, AXES, across)
    near = lax.ppermute(near, AXES, beside)
    pieces = render(far, near, inner)
    parts = lax.all_to_all(pieces, ("zh", "zl", "c"), split_axis=0, concat_axis=0, tiled=True)
    rows = run(merge_kernel, floats((64, LANES)), (), [VMEM_SPEC], 2)(parts)[0]
    rows = lax.all_to_all(rows, ("y", "x"), split_axis=0, concat_axis=0, tiled=True)
    return run(final_kernel, floats((3, 16)), (), [VMEM_SPEC], 2)(rows)[0]


def solution(mesh):
    grid = Mesh(mesh.devices.reshape(2, 8, 8, 4, 2), AXES)
    placed = (P(AXES, None, None), P(AXES, None, None), P(), P())
    return jax.shard_map(on_device, mesh=grid, in_specs=placed, out_specs=P(None, AXES), check_vma=False)
```
